32 devices in a mesh: dp: 8 (over y, x, core), fsdp: 4 (over z).
Axes of the slice: x: 2, y: 2, z: 4, core: 2. Of those that a mesh axis runs over, the one named last changes fastest.
Arguments:
- tokens_in: bfloat16 [32, 512, 1536], P(('dp', 'fsdp')), may hold values from -6 to 6
- condition: bfloat16 [32, 2, 1536], P(('dp', 'fsdp')), may hold values from -6 to 6
- item_flags: int32 [32, 512], P(('dp', 'fsdp')), may hold values from 0 to 1, as said below
- grad_out: bfloat16 [32, 512, 1536], P(('dp', 'fsdp')), may hold values from -6 to 6
- in_weight: bfloat16 [1536, 6144], P(('dp', 'fsdp')), may hold values from -0.15625 to 0.15625
- out_weight: bfloat16 [3072, 1536], P(('dp', 'fsdp')), may hold values from -0.109375 to 0.109375
- x_projection: bfloat16 [2, 3072, 128], P(None, ('dp', 'fsdp')), may hold values from -0.109375 to 0.109375
- dt_projection: bfloat16 [2, 96, 3072], P(None, None, ('dp', 'fsdp')), may hold values from -0.625 to 0.625
- conv_weight: bfloat16 [2, 4, 3072], P(None, None, ('dp', 'fsdp')), may hold values from -3 to 3
- conv_bias: bfloat16 [2, 3072], P(None, ('dp', 'fsdp')), may hold values from -4 to 4
- dt_bias: bfloat16 [2, 3072], P(None, ('dp', 'fsdp')), may hold values from -6.5 to -2.5
- decay_log: bfloat16 [2, 3072, 16], P(None, ('dp', 'fsdp')), may hold values from -0.69921875 to 2.796875
- skip_gain: bfloat16 [2, 3072], P(None, ('dp', 'fsdp')), may hold values from 0.5 to 1.5
- mod_weight: bfloat16 [1536, 4608], P(('dp', 'fsdp')), may hold values from -0.15625 to 0.15625
- mod_bias: bfloat16 [4608], P(('dp', 'fsdp')), may hold values from -4 to 4
Outputs:
- block_out: bfloat16 [32, 512, 1536], P(('dp', 'fsdp'))
- grad_tokens: float32 [32, 512, 1536], P(('dp', 'fsdp'))
- grad_condition: float32 [32, 2, 1536], P(('dp', 'fsdp'))
- grad_in_weight: float32 [1536, 6144], P(('dp', 'fsdp'))
- grad_out_weight: float32 [3072, 1536], P(('dp', 'fsdp'))
- grad_x_projection: float32 [2, 3072, 128], P(None, ('dp', 'fsdp'))
- grad_dt_projection: float32 [2, 96, 3072], P(None, None, ('dp', 'fsdp'))
- grad_conv_weight: float32 [2, 4, 3072], P(None, None, ('dp', 'fsdp'))
- grad_conv_bias: float32 [2, 3072], P(None, ('dp', 'fsdp'))
- grad_dt_bias: float32 [2, 3072], P(None, ('dp', 'fsdp'))
- grad_decay_log: float32 [2, 3072, 16], P(None, ('dp', 'fsdp'))
- grad_skip_gain: float32 [2, 3072], P(None, ('dp', 'fsdp'))
- grad_mod_weight: float32 [1536, 4608], P(('dp', 'fsdp'))
- grad_mod_bias: float32 [4608], P(('dp', 'fsdp'))
The draws below stay inside these ranges and needn't reach their ends.
Inputs may be any that keep to these rules, and one draw needn't show every extreme that they name: Each row holds two items: item_flags is 1 at position 0 and at exactly one position p with 128 <= p <= 384, and 0 elsewhere.
All inputs are finite; a program needn't handle non-finite values.
Results may differ from the reference program's by a relative error of at most 0.012.
The reference program's roundings to bfloat16 on the way count: a program that leaves them out, or rounds other values in their place, can miss the bound.
Values may be sent and summed in bfloat16 or wider, within the bound.
No kernel may reach another device: no remote copies, remote signals or barrier semaphores. Data moves between devices by JAX's collectives and lax.ppermute only.
A program may use at most 384 MiB of HBM per device.

```python
import jax
import jax.numpy as jnp
from jax import lax

D = 1536
E = 3072
NST = 16
RDT = 96
KCONV = 4
LEN = 512
SCAN_BLOCK = 32
ROWS = 32


def draw_item_flags(key, part):
    second_start = jax.random.randint(key, (ROWS, 1), LEN // 4, 3 * LEN // 4 + 1)
    position = jnp.arange(LEN, dtype=jnp.int32)[None, :]
    return jnp.logical_or(position == 0, position == second_start).astype(jnp.int32)


def spiked(entries, key, source, target, shards_of, factor):
    owner, partner = [(jnp.arange(entries.shape[axis_at]) // (entries.shape[axis_at] // shards_of)).reshape([-1 if axis == axis_at else 1 for axis in range(entries.ndim)]) for axis_at in (source, target)]
    chosen = jax.random.permutation(key, shards_of)[partner]
    strong = (owner == chosen) | (owner == (partner + shards_of // 2) % shards_of)
    return jnp.where(strong, factor * entries, entries)


def level_of(own_key, dims, cuts, smallest, largest):
    def one(dim, blocks):
        draws = jax.random.uniform(jax.random.fold_in(jax.random.fold_in(own_key, 6), dim), (blocks,), jnp.float32, smallest / len(cuts), largest / len(cuts))
        return jnp.repeat(jnp.exp(draws), dims[dim] // blocks).reshape((-1,) + (1,) * (len(dims) - dim - 1))

    level = one(*cuts[0])
    for cut in cuts[1:]:
        level = level * one(*cut)
    return level


def noise(key, shape, width, reach, pieces=(), held_as=jnp.bfloat16):
    array = width * jax.random.normal(key, shape, jnp.float32)
    if pieces:
        array = array * level_of(key, shape, pieces, -0.22, 0.18)
    return jnp.clip(array, -reach, reach).astype(held_as)


def gaussian_with(rng, shape, width, bound, split, heavy, held_as=jnp.bfloat16):
    entries = width * jax.random.normal(rng, shape, jnp.float32)
    if split:
        entries = entries * level_of(rng, shape, split, -0.22, 0.18)
    return jnp.clip(spiked(entries, jax.random.fold_in(rng, 3), *heavy), -bound, bound).astype(held_as)


def setup_inputs(seed: int = 0) -> dict:
    key_of = jax.random.split(jax.random.key(seed), 16)
    tokens_in = gaussian_with(key_of[0], (ROWS, LEN, D), 1.0, 6.0, ((0, 32),), (0, 2, 32, 2.75))
    condition = noise(key_of[1], (ROWS, 2, D), 1.0, 6.0, ((0, 32),))
    item_flags = draw_item_flags(jax.random.fold_in(key_of[15], 71), 0)
    grad_out = gaussian_with(key_of[3], (ROWS, LEN, D), 1.0, 6.0, ((0, 32),), (0, 2, 32, 2.75))
    in_weight = noise(key_of[4], (D, 2 * E), D ** -0.5, 0.15625, ((0, 32),))
    out_weight = noise(key_of[5], (E, D), E ** -0.5, 0.109375, ((0, 32),))
    x_projection = noise(key_of[6], (2, E, RDT + 2 * NST), E ** -0.5, 0.109375, ((1, 32),))
    dt_projection = noise(key_of[7], (2, RDT, E), RDT ** -0.5, 0.625, ((2, 32),))
    conv_weight = noise(key_of[8], (2, KCONV, E), KCONV ** -0.5, 3.0, ((2, 32),))
    conv_bias = noise(key_of[9], (2, E), 0.3, 4.0, ((1, 32),))
    dt_bias = jnp.clip(-6.5 + 4.0 * jax.random.uniform(key_of[10], (2, E), jnp.float32) ** level_of(key_of[10], (2, E), ((1, 32),), -0.2, 0.2), -6.5, -2.5).astype(jnp.bfloat16)
    decay_log = jnp.clip(-0.69921875 + 3.4960938 * jax.random.uniform(key_of[11], (2, E, NST), jnp.float32) ** level_of(key_of[11], (2, E, NST), ((1, 32),), -0.2, 0.2), -0.69921875, 2.796875).astype(jnp.bfloat16)
    skip_gain = jnp.clip(0.5 + 1.0 * jax.random.uniform(key_of[12], (2, E), jnp.float32) ** level_of(key_of[12], (2, E), ((1, 32),), -0.2, 0.2), 0.5, 1.5).astype(jnp.bfloat16)
    mod_weight = noise(key_of[13], (D, 3 * D), D ** -0.5, 0.15625, ((0, 32),))
    mod_bias = noise(key_of[14], (3 * D,), 0.3, 4.0, ((0, 32),))
    return {"tokens_in": tokens_in, "condition": condition, "item_flags": item_flags, "grad_out": grad_out, "in_weight": in_weight, "out_weight": out_weight, "x_projection": x_projection, "dt_projection": dt_projection, "conv_weight": conv_weight, "conv_bias": conv_bias, "dt_bias": dt_bias, "decay_log": decay_log, "skip_gain": skip_gain, "mod_weight": mod_weight, "mod_bias": mod_bias}


@jax.custom_vjp
def low(v):
    return lax.optimization_barrier(v.astype(jnp.bfloat16)).astype(jnp.float32)

@jax.custom_vjp
def low_back(v):
    return v

def low_keep(v):
    return (low(v), None)

def low_pass(kept, grad):
    return (grad,)

def back_keep(v):
    return (v, None)

def back_low(kept, grad):
    return (low(grad),)
low.defvjp(low_keep, low_pass)
low_back.defvjp(back_keep, back_low)
norm_eps = 1e-06
highest = lax.Precision.HIGHEST

def combine(first, second):
    return (first[0] * second[0], second[0] * first[1] + second[1])

def scan_row(values, deltas, b_matrix, c_matrix, decay_rate, skip_row, starts):
    block_count = values.shape[0] // SCAN_BLOCK

    def block_step(carry_state, pieces_now):
        value_blk, delta_blk, b_blk, c_blk, start_blk = pieces_now
        decays = jnp.exp(delta_blk[:, :, None] * decay_rate[None]) * (1.0 - start_blk)[:, None, None]
        drives = (delta_blk * value_blk)[:, :, None] * b_blk[:, None, :]
        acc_decay, acc_drive = lax.associative_scan(combine, (decays, drives), axis=0)
        states = acc_decay * carry_state[None] + acc_drive
        result = lax.optimization_barrier(jnp.sum(states * c_blk[:, None, :], axis=2)) + skip_row * value_blk
        return (states[-1], result)
    blocks = tuple((item.reshape((block_count, SCAN_BLOCK) + item.shape[1:]) for item in (values, deltas, b_matrix, c_matrix, starts)))
    start_state = jnp.zeros((values.shape[1], b_matrix.shape[1]), values.dtype)
    _, results = lax.scan(jax.checkpoint(block_step), start_state, blocks)
    return results.reshape(values.shape)

def run_scans(values, dt_raw, b_and_c, bias_dt, log_rate, skips, both_starts):
    deltas = jax.nn.softplus(dt_raw + bias_dt[:, None, None, :])
    rates = -jnp.exp(log_rate)
    b_matrix = b_and_c[..., :NST]
    c_matrix = b_and_c[..., NST:]
    outputs = []
    for direction in range(2):

        def one_row(row_args, direction=direction):
            return scan_row(row_args[0], row_args[1], row_args[2], row_args[3], rates[direction], skips[direction], row_args[4])
        outputs.append(lax.map(one_row, (values[direction], deltas[direction], b_matrix[direction], c_matrix[direction], both_starts[direction])))
    return jnp.stack(outputs)

def conv_silu(values, weights, conv_shift, starts):
    ids_now = jnp.cumsum(starts, axis=1, dtype=jnp.int32)
    length = values.shape[1]
    padded = jnp.pad(values, ((0, 0), (KCONV - 1, 0), (0, 0)))
    padded_ids = jnp.pad(ids_now, ((0, 0), (KCONV - 1, 0)), constant_values=-1)
    summed = values * weights[0] + conv_shift
    for lag_index in range(1, KCONV):
        offset = KCONV - 1 - lag_index
        seen_rows = padded[:, offset:offset + length]
        same_item = (padded_ids[:, offset:offset + length] == ids_now)[:, :, None]
        summed = summed + weights[lag_index] * jnp.where(same_item, seen_rows, 0.0)
    return jax.nn.silu(summed)

def conv_both(both_x, weights, biases, both_starts):
    return jnp.stack([conv_silu(both_x[direction], weights[direction], biases[direction], both_starts[direction]) for direction in range(2)])

def reverse_starts(starts):
    flipped = jnp.flip(starts, axis=1)
    first_col = jnp.ones_like(starts[:, :1])
    return jnp.concatenate([first_col, flipped[:, :-1]], axis=1)

def per_token(modulation, ids_now):
    second_item = (ids_now == 1)[:, :, None]
    return jnp.where(second_item, modulation[:, 1][:, None, :], modulation[:, 0][:, None, :])

def normalize(x_now):
    row_mean = lax.optimization_barrier(jnp.mean(x_now, axis=-1, keepdims=True))
    centered = x_now - row_mean
    variance = lax.optimization_barrier(jnp.mean(centered * centered, axis=-1, keepdims=True))
    return centered * lax.rsqrt(variance + norm_eps)

def front(x_now, modulation, ids_now):
    model_width = x_now.shape[-1]
    shift_tok = per_token(modulation[..., :model_width], ids_now)
    scale_tok = per_token(modulation[..., model_width:2 * model_width], ids_now)
    return normalize(x_now) * (1.0 + scale_tok) + shift_tok

def finish(x_now, modulation, branch, ids_now):
    model_width = x_now.shape[-1]
    gate_tok = per_token(modulation[..., 2 * model_width:], ids_now)
    return x_now + gate_tok * branch

def combine_ways(scan_outs, z_part):
    return (scan_outs[0] + jnp.flip(scan_outs[1], axis=1)) * jax.nn.silu(z_part)

def forward(params, x_now, cond_now, starts):
    in_weight, out_weight, x_projection, dt_projection, conv_weight, conv_bias, dt_bias, decay_log, skip_gain, mod_weight, mod_bias = params
    ids_now = jnp.cumsum(starts, axis=1, dtype=jnp.int32) - 1
    cond_act = low(jax.nn.silu(cond_now))
    modulation = low_back(jnp.einsum('rid,dk->rik', cond_act, mod_weight, precision=highest)) + mod_bias
    hidden = low(front(x_now, modulation, ids_now))
    mixed_rows = low_back(jnp.einsum('rtd,dk->rtk', hidden, in_weight, precision=highest))
    inner_width = mixed_rows.shape[-1] // 2
    x_part = mixed_rows[..., :inner_width]
    z_part = mixed_rows[..., inner_width:]
    both_starts = jnp.stack([starts, reverse_starts(starts)])
    both_x = jnp.stack([x_part, jnp.flip(x_part, axis=1)])
    conv_out = low(conv_both(both_x, conv_weight, conv_bias, both_starts))
    projected = low_back(jnp.einsum('grte,gek->grtk', conv_out, x_projection, precision=highest))
    dt_low = low(projected[..., :RDT])
    dt_raw = low_back(jnp.einsum('grtk,gke->grte', dt_low, dt_projection, precision=highest))
    scan_outs = run_scans(conv_out, dt_raw, projected[..., RDT:], dt_bias, decay_log, skip_gain, both_starts.astype(x_now.dtype))
    gated = low(combine_ways(scan_outs, z_part))
    branch = low_back(jnp.einsum('rte,ed->rtd', gated, out_weight, precision=highest))
    return finish(x_now, modulation, branch, ids_now)

def reference(tokens_in, condition, item_flags, grad_out, in_weight, out_weight, x_projection, dt_projection, conv_weight, conv_bias, dt_bias, decay_log, skip_gain, mod_weight, mod_bias):
    params = tuple((item.astype(jnp.float32) for item in (in_weight, out_weight, x_projection, dt_projection, conv_weight, conv_bias, dt_bias, decay_log, skip_gain, mod_weight, mod_bias)))
    group_rows = 8
    group_count = ROWS // group_rows

    def split_rows(item):
        return item.reshape((group_count, group_rows) + item.shape[1:])

    def group_step(totals, batch):
        x_grp, cond_grp, flags_grp, grad_grp = batch

        def local_forward(params_now, x_now, cond_now):
            return forward(params_now, x_now, cond_now, flags_grp)
        out_grp, pull_back = jax.vjp(local_forward, params, x_grp.astype(jnp.float32), cond_grp.astype(jnp.float32))
        d_params, d_x, d_cond = pull_back(grad_grp.astype(jnp.float32))
        totals = jax.tree.map(jnp.add, totals, d_params)
        return (totals, (out_grp.astype(jnp.bfloat16), d_x, d_cond))
    zero_grads = jax.tree.map(jnp.zeros_like, params)
    totals, stacked = lax.scan(group_step, zero_grads, (split_rows(tokens_in), split_rows(condition), split_rows(item_flags), split_rows(grad_out)))
    out_rows = stacked[0].reshape(tokens_in.shape)
    grad_tokens = stacked[1].reshape(tokens_in.shape)
    grad_condition = stacked[2].reshape(condition.shape)
    return (out_rows, grad_tokens, grad_condition, totals[0], totals[1], totals[2], totals[3], totals[4], totals[5], totals[6], totals[7], totals[8], totals[9], totals[10])
```

```python
import functools

import jax
import jax.numpy as jnp
from jax import lax
from jax.experimental import pallas as pl
from jax.experimental.pallas import tpu as pltpu
from jax.sharding import PartitionSpec as P

NST = 16
SUB = 16
LANES = 128
bf16 = jnp.bfloat16
f32 = jnp.float32


def split_hi_lo(v):
    hi = v.astype(bf16)
    lo = (v - hi.astype(f32)).astype(bf16)
    return jnp.concatenate([hi, lo], axis=0)


def block_diag(tiled):
    rows = lax.broadcasted_iota(jnp.int32, tiled.shape, 0)
    cols = lax.broadcasted_iota(jnp.int32, tiled.shape, 1) // NST
    return jnp.where(rows == cols, tiled, 0.0)


def fwd_kernel(delta_ref, u_ref, sb_ref, bx_ref, ct_ref, a2_ref, skip_ref, y_ref, ck_ref,
               h_scr, dx_scr, du_scr, hs_scr, *, backwards, subs, width):
    first = pl.program_id(1) == 0
    lane0 = pl.multiple_of(pl.program_id(2) * width, width)
    tiles = width // LANES

    @pl.when(first)
    def _():
        h_scr[:, pl.ds(lane0, width)] = jnp.zeros((NST, width), f32)

    order = range(SUB - 1, -1, -1) if backwards else range(SUB)

    def sub_step(step, carry):
        sub = subs - 1 - step if backwards else step
        row0 = pl.multiple_of(sub * SUB, SUB)
        rows = pl.ds(row0, SUB)
        delta = delta_ref[rows, :]
        u = u_ref[rows, :].astype(f32)
        du_scr[...] = delta * u
        sb = sb_ref[rows, :]
        for j in range(tiles):
            lanes = pl.ds(j * LANES, LANES)
            dx_scr[:, lanes] = delta[:, j * LANES:(j + 1) * LANES] + sb
        h = [h_scr[:, pl.ds(lane0 + j * LANES, LANES)] for j in range(tiles)]
        a2 = [a2_ref[:, pl.ds(lane0 + j * LANES, LANES)] for j in range(tiles)]
        for j in range(tiles):
            ck_ref[sub, :, pl.ds(j * LANES, LANES)] = h[j]
        for t in order:
            b = bx_ref[row0 + t]
            for j in range(tiles):
                lanes = pl.ds(j * LANES, LANES)
                dx = dx_scr[pl.ds(t, 1), lanes]
                du = du_scr[pl.ds(t, 1), lanes]
                h[j] = jnp.exp2(dx * a2[j]) * h[j] + du * b
                hs_scr[pl.ds(t * NST, NST), lanes] = h[j].astype(bf16)
        for j in range(tiles):
            h_scr[:, pl.ds(lane0 + j * LANES, LANES)] = h[j]
        c2 = split_hi_lo(block_diag(ct_ref[rows, :]))
        y2 = jnp.dot(c2, hs_scr[...], preferred_element_type=f32)
        y_ref[rows, :] = y2[:SUB] + y2[SUB:] + skip_ref[:, pl.ds(lane0, width)] * u
        return carry

    lax.fori_loop(0, subs, sub_step, 0)


def bwd_kernel(delta_ref, u_ref, sb_ref, bx_ref, cx_ref, bt_ref, ds_ref, ck_ref, a_ref, a2_ref,
               skip_ref, du_out, dr_out, db_out, dc_out, ga_out, gs_out, gb_out,
               g_scr, dx_scr, du_scr, ds_scr, da_scr, hp_scr, hs_scr, lam_scr, r_scr,
               *, backwards, subs, width):
    first = pl.program_id(1) == 0
    start = jnp.logical_and(first, pl.program_id(0) == 0)
    eg = pl.program_id(2)
    lane0 = pl.multiple_of(eg * width, width)
    tiles = width // LANES
    wide = pl.ds(lane0, width)

    @pl.when(first)
    def _():
        g_scr[:, wide] = jnp.zeros((NST, width), f32)

    @pl.when(start)
    def _():
        ga_out[:, wide] = jnp.zeros((NST, width), f32)
        gs_out[:, wide] = jnp.zeros((SUB, width), f32)
        gb_out[:, wide] = jnp.zeros((SUB, width), f32)

    @pl.when(eg == 0)
    def _():
        db_out[...] = jnp.zeros_like(db_out)
        dc_out[...] = jnp.zeros_like(dc_out)

    order = list(range(SUB - 1, -1, -1) if backwards else range(SUB))

    def sub_step(step, carry):
        sub = step if backwards else subs - 1 - step
        row0 = pl.multiple_of(sub * SUB, SUB)
        rows = pl.ds(row0, SUB)
        delta = delta_ref[rows, :]
        u = u_ref[rows, :].astype(f32)
        ds = ds_ref[rows, :]
        du_scr[...] = delta * u
        ds_scr[...] = ds
        sb = sb_ref[rows, :]
        for j in range(tiles):
            dx_scr[:, pl.ds(j * LANES, LANES)] = delta[:, j * LANES:(j + 1) * LANES] + sb
        for j in range(tiles):
            lanes = pl.ds(j * LANES, LANES)
            a2 = a2_ref[:, pl.ds(lane0 + j * LANES, LANES)]
            h = ck_ref[sub, :, lanes]
            for t in order:
                dx = dx_scr[pl.ds(t, 1), lanes]
                du = du_scr[pl.ds(t, 1), lanes]
                hp_scr[t, :, lanes] = h
                da = jnp.exp2(dx * a2)
                da_scr[t, :, lanes] = da
                h = da * h + du * bx_ref[row0 + t]
                hs_scr[pl.ds(t * NST, NST), lanes] = h.astype(bf16)
        for j in range(tiles):
            lanes = pl.ds(j * LANES, LANES)
            glob = pl.ds(lane0 + j * LANES, LANES)
            a = a_ref[:, glob]
            g = g_scr[:, glob]
            ga = ga_out[:, glob]
            for t in reversed(order):
                lam = cx_ref[row0 + t] * ds_scr[pl.ds(t, 1), lanes] + g
                lam_scr[pl.ds(t * NST, NST), lanes] = lam.astype(bf16)
                g = da_scr[t, :, lanes] * lam
                r = g * hp_scr[t, :, lanes] * a
                r_scr[pl.ds(t * NST, NST), lanes] = r.astype(bf16)
                ga = ga + dx_scr[pl.ds(t, 1), lanes] * r
            g_scr[:, glob] = g
            ga_out[:, glob] = ga
        b2 = split_hi_lo(block_diag(bt_ref[rows, :]))
        s2 = jnp.dot(b2, lam_scr[...], preferred_element_type=f32)
        s1 = s2[:SUB] + s2[SUB:]
        ones = block_diag(jnp.ones((SUB, SUB * NST), f32)).astype(bf16)
        dd = jnp.dot(ones, r_scr[...], preferred_element_type=f32) + u * s1
        du_out[rows, :] = skip_ref[:, wide] * ds + delta * s1
        small = delta * (1.0 - delta * (0.5 - delta * (1.0 / 6.0)))
        sig = jnp.where(delta < 0.03, small, 1.0 - jnp.exp(-delta))
        dr = dd * sig
        dr_out[rows, :] = dr.astype(bf16)
        gb_out[:, wide] += dr
        gs_out[:, wide] += ds * u
        nt = (((1,), (1,)), ((), ()))
        d2 = lax.dot_general(split_hi_lo(delta * u), lam_scr[...], nt, preferred_element_type=f32)
        db_out[rows, :] += d2[:SUB] + d2[SUB:]
        e2 = lax.dot_general(split_hi_lo(ds), hs_scr[...], nt, preferred_element_type=f32)
        dc_out[rows, :] += e2[:SUB] + e2[SUB:]
        return carry

    lax.fori_loop(0, subs, sub_step, 0)


def lane_groups(width_all):
    for width in (512, 384, 256, 128):
        if width_all % width == 0:
            return width
    return width_all


def scan_calls(rows, length, inner, backwards, tblock=128, width=None):
    width = width or lane_groups(inner)
    n_t, n_e, subs = length // tblock, inner // width, tblock // SUB
    params = pltpu.CompilerParams(dimension_semantics=("arbitrary",) * 3)

    def specs(flip):
        tb = (lambda i: n_t - 1 - i) if flip else (lambda i: i)
        tok = pl.BlockSpec((None, tblock, width), lambda r, i, e: (r, tb(i), e))
        lane = pl.BlockSpec((None, tblock, LANES), lambda r, i, e: (r, tb(i), 0))
        exp = pl.BlockSpec((None, tblock, NST, LANES), lambda r, i, e: (r, tb(i), 0, 0))
        til = pl.BlockSpec((None, tblock, SUB * NST), lambda r, i, e: (r, tb(i), 0))
        ck = pl.BlockSpec((None, subs, NST, width), lambda r, i, e: (r, tb(i), 0, e))
        full = pl.BlockSpec((NST, inner), lambda r, i, e: (0, 0))
        one = pl.BlockSpec((1, inner), lambda r, i, e: (0, 0))
        return tok, lane, exp, til, ck, full, one

    sds = jax.ShapeDtypeStruct
    work = rows * length * inner * NST
    tok, lane, exp, til, ck, full, one = specs(backwards)
    fwd = pl.pallas_call(
        functools.partial(fwd_kernel, backwards=backwards, subs=subs, width=width),
        grid=(rows, n_t, n_e),
        in_specs=[tok, tok, lane, exp, til, full, one],
        out_specs=[tok, ck],
        out_shape=[sds((rows, length, inner), f32), sds((rows, length // SUB, NST, inner), f32)],
        scratch_shapes=[pltpu.VMEM((NST, inner), f32), pltpu.VMEM((SUB, width), f32),
                        pltpu.VMEM((SUB, width), f32), pltpu.VMEM((SUB * NST, width), bf16)],
        compiler_params=params,
        name="scan_ahead_" + ("b" if backwards else "f"),
    )
    tok, lane, exp, til, ck, full, one = specs(not backwards)
    bwd = pl.pallas_call(
        functools.partial(bwd_kernel, backwards=backwards, subs=subs, width=width),
        grid=(rows, n_t, n_e),
        in_specs=[tok, tok, lane, exp, exp, til, tok, ck, full, full, one],
        out_specs=[tok, tok, til, til, full, full, full],
        out_shape=[sds((rows, length, inner), f32), sds((rows, length, inner), bf16),
                   sds((rows, length, SUB * NST), f32), sds((rows, length, SUB * NST), f32),
                   sds((NST, inner), f32), sds((SUB, inner), f32), sds((SUB, inner), f32)],
        scratch_shapes=[pltpu.VMEM((NST, inner), f32)] + [pltpu.VMEM((SUB, width), f32)] * 3
        + [pltpu.VMEM((SUB, NST, width), f32)] * 2 + [pltpu.VMEM((SUB * NST, width), bf16)] * 3,
        compiler_params=params,
        name="scan_back_" + ("b" if backwards else "f"),
    )
    return fwd, bwd


RDT = 96
KCONV = 4
EPS = 1e-06
AXES = ("dp", "fsdp")
BIG = 1e30
LOG2E = 1.4426950408889634


def shifted(v, by):
    if by == 0:
        return v
    pad = jnp.zeros((abs(by),) + v.shape[1:], v.dtype)
    if by > 0:
        return jnp.concatenate([pad, v[:-by]], axis=0)
    return jnp.concatenate([v[-by:], pad], axis=0)


def same_item(ids, by):
    return (shifted(ids + 1, by) == ids + 1)[:, None]


def conv_pre(x, weights, bias, ids, sign):
    pre = x * weights[0] + bias
    for lag in range(1, KCONV):
        pre = pre + weights[lag] * jnp.where(same_item(ids, sign * lag), shifted(x, sign * lag), 0.0)
    return pre


def mm(a, b, dims):
    return lax.dot_general(a, b, (dims, ((), ())), preferred_element_type=f32)


def body(tokens_in, condition, item_flags, grad_out, in_weight, out_weight, x_projection,
         dt_projection, conv_weight, conv_bias, dt_bias, decay_log, skip_gain, mod_weight, mod_bias):
    length, model = tokens_in.shape[1:]
    owners = lax.axis_size(AXES)
    me = lax.axis_index(AXES)
    inner = in_weight.shape[1] // 2
    own_model = in_weight.shape[0]
    own_inner = out_weight.shape[0]
    gather0 = lambda v: lax.all_gather(v, AXES, axis=0, tiled=True)

    cond = condition[0].astype(f32)
    act = jax.nn.silu(cond).astype(bf16)
    smalls = (act, conv_weight, conv_bias, dt_bias, decay_log, skip_gain, mod_bias)
    flat = jnp.concatenate([v.reshape(-1) for v in smalls])
    flat = jnp.pad(flat, (0, -flat.shape[0] % LANES))
    everyone = lax.all_gather(flat, AXES, axis=0, tiled=False)
    parts, at = [], 0
    for v in smalls:
        parts.append(everyone[:, at:at + v.size].reshape((owners,) + v.shape))
        at += v.size
    act_all = parts[0].reshape(owners * 2, model)
    join = lambda v, dim: jnp.moveaxis(v, 0, dim).reshape(
        v.shape[1:dim + 1] + (owners * v.shape[dim + 1],) + v.shape[dim + 2:]).astype(f32)
    conv_w, conv_b, dt_b = join(parts[1], 2), join(parts[2], 1), join(parts[3], 1)
    log_rate, skip = join(parts[4], 1), join(parts[5], 1)
    modb = parts[6].reshape(-1).astype(f32)

    w_x = gather0(in_weight[:, :inner])
    w_xp = lax.all_gather(x_projection, AXES, axis=1, tiled=True)
    w_dt = lax.all_gather(dt_projection, AXES, axis=2, tiled=True)
    w_z = gather0(in_weight[:, inner:])
    w_o = gather0(out_weight)

    act_own = lax.dynamic_slice(act_all, (0, me * own_model), (owners * 2, own_model))
    partial = mm(act_own, mod_weight, ((1,), (0,))).reshape(owners, 2, -1)
    mods = jnp.sum(lax.all_to_all(partial, AXES, 0, 0, tiled=True), axis=0) + modb
    flags = item_flags[0]
    ids = jnp.cumsum(flags, dtype=jnp.int32) - 1
    second = (ids == 1)[:, None]
    pick = lambda v: jnp.where(second, v[1], v[0])
    shift, scale, gate = (mods[:, i * model:(i + 1) * model] for i in range(3))

    x = tokens_in[0].astype(f32)
    mean = jnp.mean(x, axis=1, keepdims=True)
    centered = x - mean
    inv = lax.rsqrt(jnp.mean(centered * centered, axis=1, keepdims=True) + EPS)
    normed = centered * inv
    hidden = (normed * (1.0 + pick(scale)) + pick(shift)).astype(bf16)
    xs = mm(hidden, w_x, ((1,), (0,)))

    g = grad_out[0].astype(f32)
    d_branch = (g * pick(gate)).astype(bf16)

    starts = flags.astype(f32)
    starts_b = jnp.concatenate([starts[1:], jnp.ones((1,), f32)])
    calls = [scan_calls(1, length, inner, bool(d)) for d in range(2)]
    wide = lambda v: jnp.broadcast_to(v[None, :, :, None], (1, length, NST, LANES))
    tile = lambda v: jnp.tile(v, (1, SUB))[None]
    kept = []
    for d, sign in ((0, 1), (1, -1)):
        u = jax.nn.silu(conv_pre(xs, conv_w[d], conv_b[d], ids, sign)).astype(bf16)
        proj = mm(u, w_xp[d], ((1,), (0,)))
        dt_low = proj[:, :RDT].astype(bf16)
        b_m, c_m = proj[:, RDT:RDT + NST], proj[:, RDT + NST:]
        delta = jax.nn.softplus(mm(dt_low, w_dt[d], ((1,), (0,))) + dt_b[d])
        rate = -jnp.exp(log_rate[d]).T
        rate2 = rate * LOG2E
        sb = jnp.broadcast_to((BIG * (starts_b if d else starts))[None, :, None], (1, length, LANES))
        b_wide = wide(b_m)
        y, ck = calls[d][0](delta[None], u[None], sb, b_wide, tile(c_m), rate2, skip[d][None])
        kept.append((u, dt_low, b_m, c_m, delta, rate, rate2, sb, b_wide, y[0], ck))
    both = kept[0][9] + kept[1][9]
    z = mm(hidden, w_z, ((1,), (0,)))
    sig_z = jax.nn.sigmoid(z)
    silu_z = z * sig_z
    gated = (both * silu_z).astype(bf16)
    branch = mm(gated, w_o, ((1,), (0,)))
    block_out = (x + pick(gate) * branch).astype(bf16)

    d_gate = g * branch
    scatter = lambda v: lax.psum_scatter(v, AXES, scatter_dimension=0, tiled=True)
    grad_out_w = scatter(mm(gated, d_branch, ((0,), (0,))).astype(bf16)).astype(f32)
    d_gated = mm(d_branch, w_o, ((1,), (1,)))
    d_scan = d_gated * silu_z
    d_z = (d_gated * both * sig_z * (1.0 + z * (1.0 - sig_z))).astype(bf16)
    grad_in_z = scatter(mm(hidden, d_z, ((0,), (0,))).astype(bf16)).astype(f32)
    d_xs = 0.0
    per_dir = []
    for d, sign in ((0, 1), (1, -1)):
        u, dt_low, b_m, c_m, delta, rate, rate2, sb, b_wide, _, ck = kept[d]
        du, dr, db, dc, ga, gs, gb = calls[d][1](
            delta[None], u[None], sb, b_wide, wide(c_m), tile(b_m), d_scan[None], ck, rate, rate2,
            skip[d][None])
        own = lambda m: jnp.sum(jnp.where(
            jnp.eye(SUB, dtype=bool)[None, :, :, None],
            m.reshape(length // SUB, SUB, SUB, NST), 0.0), axis=2).reshape(length, NST)
        dr = dr[0]
        g_dt = mm(dt_low, dr, ((0,), (0,)))
        d_low = mm(dr, w_dt[d], ((1,), (1,)))
        d_proj = jnp.concatenate([d_low, own(db), own(dc)], axis=1).astype(bf16)
        g_xp = mm(u, d_proj, ((0,), (0,)))
        d_u = du[0] + mm(d_proj, w_xp[d], ((1,), (1,)))
        pre = conv_pre(xs, conv_w[d], conv_b[d], ids, sign)
        sg = jax.nn.sigmoid(pre)
        d_pre = d_u * sg * (1.0 + pre * (1.0 - sg))
        g_cb = jnp.sum(d_pre, axis=0)
        g_cw = []
        for lag in range(KCONV):
            mine = jnp.where(same_item(ids, sign * lag), shifted(xs, sign * lag), 0.0) if lag else xs
            g_cw.append(jnp.sum(d_pre * mine, axis=0))
            back = (jnp.where(same_item(ids, -sign * lag), shifted(d_pre, -sign * lag), 0.0)
                    if lag else d_pre)
            d_xs = d_xs + conv_w[d, lag] * back
        per_dir.append((g_xp, g_dt, jnp.stack(g_cw), g_cb, jnp.sum(gb, axis=0), ga.T,
                        jnp.sum(gs, axis=0)))
    d_xs = d_xs.astype(bf16)
    grad_in_x = scatter(mm(hidden, d_xs, ((0,), (0,))).astype(bf16)).astype(f32)
    grad_in = jnp.concatenate([grad_in_x, grad_in_z], axis=1)
    d_hidden = mm(d_xs, w_x, ((1,), (1,))) + mm(d_z, w_z, ((1,), (1,)))

    stacked = [jnp.stack(pair) for pair in zip(*per_dir)]
    dims = (1, 2, 2, 1, 1, 1, 1)
    pieces, shapes = [], []
    for v, dim in zip(stacked, dims):
        shape = v.shape[:dim] + (owners, v.shape[dim] // owners) + v.shape[dim + 1:]
        pieces.append(jnp.moveaxis(v.reshape(shape), dim, 0).reshape(owners, -1).astype(bf16))
        shapes.append(v.shape[:dim] + (v.shape[dim] // owners,) + v.shape[dim + 1:])
    packed = jnp.concatenate(pieces, axis=1)
    packed = jnp.pad(packed, ((0, 0), (0, -packed.shape[1] % (16 * LANES))))
    mine = scatter(packed.reshape(-1, LANES)).astype(f32).reshape(-1)
    small_grads, at = [], 0
    for shape in shapes:
        count = 1
        for n in shape:
            count *= n
        small_grads.append(mine[at:at + count].reshape(shape))
        at += count

    scale_tok = 1.0 + pick(scale)
    d_n = d_hidden * scale_tok
    m1 = jnp.mean(d_n, axis=1, keepdims=True)
    m2 = jnp.mean(d_n * normed, axis=1, keepdims=True)
    grad_tokens = g + (d_n - m1 - normed * m2) * inv
    by_item = lambda v: jnp.stack([jnp.sum(jnp.where(second, 0.0, v), axis=0),
                                   jnp.sum(jnp.where(second, v, 0.0), axis=0)])
    d_mods = jnp.concatenate([by_item(d_hidden), by_item(d_hidden * normed), by_item(d_gate)], axis=1)
    d_mods_all = gather0(d_mods.astype(bf16))
    grad_mod_w = mm(act_own, d_mods_all, ((0,), (0,)))
    own_b = mod_bias.shape[0]
    grad_mod_b = jnp.sum(
        lax.dynamic_slice(d_mods_all, (0, me * own_b), (owners * 2, own_b)).astype(f32), axis=0)
    d_act = mm(d_mods_all, mod_weight, ((1,), (1,))).reshape(owners, 2, own_model)
    d_act = lax.all_to_all(d_act, AXES, 0, 0, tiled=True)
    d_act = jnp.moveaxis(d_act, 0, 1).reshape(2, model)
    sc = jax.nn.sigmoid(cond)
    grad_cond = d_act * sc * (1.0 + cond * (1.0 - sc))
    g_xp, g_dt, g_cw, g_cb, g_db, g_al, g_sk = small_grads
    return (block_out[None], grad_tokens[None], grad_cond[None], grad_in, grad_out_w, g_xp, g_dt,
            g_cw, g_cb, g_db, g_al, g_sk, grad_mod_w, grad_mod_b)


def solution(mesh):
    row3, row2, row1 = P(AXES, None, None), P(AXES, None), P(AXES)
    mid3, mid2, last3 = P(None, AXES, None), P(None, AXES), P(None, None, AXES)
    weights = (row2, row2, mid3, last3, last3, mid2, mid2, mid3, mid2, row2, row1)
    return jax.shard_map(
        body, mesh=mesh, in_specs=(row3, row3, row2, row3) + weights,
        out_specs=(row3, row3, row3) + weights, check_vma=False)
```

```python
import functools

import jax
import jax.numpy as jnp
from jax import lax
from jax.experimental import pallas as pl
from jax.experimental.pallas import tpu as pltpu
from jax.sharding import PartitionSpec as P

NST = 16
SUB = 16
KCONV = 4
LANES = 128
bf16 = jnp.bfloat16
f32 = jnp.float32


def split_hi_lo(v):
    hi = v.astype(bf16)
    lo = (v - hi.astype(f32)).astype(bf16)
    return jnp.concatenate([hi, lo], axis=0)


def block_diag(tiled):
    rows = lax.broadcasted_iota(jnp.int32, tiled.shape, 0)
    cols = lax.broadcasted_iota(jnp.int32, tiled.shape, 1) // NST
    return jnp.where(rows == cols, tiled, 0.0)


PAIR = 256


def fold(v):
    v = block_diag(v)
    v = v[:, :LANES] + v[:, LANES:]
    for by in (64, 32, 16):
        v = v + pltpu.roll(v, by, 1)
    return v


def fwd_kernel(delta_ref, u_ref, sb_ref, bx_ref, ct_ref, a2_ref, skip_ref, y_ref, ck_ref,
               h_scr, dx_scr, du_scr, *, backwards, subs, width):
    lane0 = pl.multiple_of(pl.program_id(2) * width, width)

    @pl.when(pl.program_id(1) == 0)
    def _():
        h_scr[:, pl.ds(lane0, width)] = jnp.zeros((NST, width), f32)

    order = range(SUB - 1, -1, -1) if backwards else range(SUB)

    def sub_step(step, carry):
        sub = subs - 1 - step if backwards else step
        row0 = pl.multiple_of(sub * SUB, SUB)
        rows = pl.ds(row0, SUB)
        sb = sb_ref[rows, :]
        sb = jnp.concatenate([sb] * (PAIR // LANES), axis=1)
        c2 = split_hi_lo(block_diag(ct_ref[rows, :]))
        for p in range(width // PAIR):
            lanes = pl.ds(p * PAIR, PAIR)
            glob = pl.ds(lane0 + p * PAIR, PAIR)
            delta = delta_ref[rows, lanes]
            u = u_ref[rows, lanes].astype(f32)
            du_scr[:, lanes] = delta * u
            dx_scr[:, lanes] = delta + sb
            h = h_scr[:, glob]
            a2 = a2_ref[:, glob]
            ck_ref[sub, :, lanes] = h
            states = [None] * SUB
            for t in order:
                b = bx_ref[row0 + t]
                b = jnp.concatenate([b] * (PAIR // LANES), axis=1)
                h = jnp.exp2(dx_scr[pl.ds(t, 1), lanes] * a2) * h + du_scr[pl.ds(t, 1), lanes] * b
                states[t] = h.astype(bf16)
            h_scr[:, glob] = h
            y2 = jnp.dot(c2, jnp.concatenate(states, axis=0), preferred_element_type=f32)
            y_ref[rows, lanes] = y2[:SUB] + y2[SUB:] + skip_ref[:, glob] * u
        return carry

    lax.fori_loop(0, subs, sub_step, 0)


def bwd_kernel(delta_ref, u_ref, sb_ref, bx_ref, cx_ref, bt_ref, ds_ref, ck_ref, a_ref, a2_ref,
               skip_ref, du_out, dr_out, db_out, dc_out, ga_out, gs_out, gb_out,
               g_scr, dx_scr, du_scr, *, backwards, subs, width):
    first = pl.program_id(1) == 0
    start = jnp.logical_and(first, pl.program_id(0) == 0)
    eg = pl.program_id(2)
    lane0 = pl.multiple_of(eg * width, width)
    wide = pl.ds(lane0, width)

    @pl.when(first)
    def _():
        g_scr[:, wide] = jnp.zeros((NST, width), f32)

    @pl.when(start)
    def _():
        ga_out[:, wide] = jnp.zeros((NST, width), f32)
        gs_out[:, wide] = jnp.zeros((SUB, width), f32)
        gb_out[:, wide] = jnp.zeros((SUB, width), f32)

    @pl.when(eg == 0)
    def _():
        db_out[...] = jnp.zeros_like(db_out)
        dc_out[...] = jnp.zeros_like(dc_out)

    order = list(range(SUB - 1, -1, -1) if backwards else range(SUB))
    nt = (((1,), (1,)), ((), ()))
    twice = lambda v: jnp.concatenate([v] * (PAIR // LANES), axis=1)

    def sub_step(step, carry):
        sub = step if backwards else subs - 1 - step
        row0 = pl.multiple_of(sub * SUB, SUB)
        rows = pl.ds(row0, SUB)
        sb = twice(sb_ref[rows, :])
        b2 = split_hi_lo(block_diag(bt_ref[rows, :]))
        ones = block_diag(jnp.ones((SUB, SUB * NST), f32)).astype(bf16)
        db, dc = jnp.zeros((SUB, SUB * NST), f32), jnp.zeros((SUB, SUB * NST), f32)
        for p in range(width // PAIR):
            lanes = pl.ds(p * PAIR, PAIR)
            glob = pl.ds(lane0 + p * PAIR, PAIR)
            delta = delta_ref[rows, lanes]
            u = u_ref[rows, lanes].astype(f32)
            ds = ds_ref[rows, lanes]
            d_in = delta * u
            du_scr[:, lanes] = d_in
            dx_scr[:, lanes] = delta + sb
            a2 = a2_ref[:, glob]
            h = ck_ref[sub, :, lanes]
            prev, decay, states = [None] * SUB, [None] * SUB, [None] * SUB
            for t in order:
                prev[t] = h
                decay[t] = jnp.exp2(dx_scr[pl.ds(t, 1), lanes] * a2)
                h = decay[t] * h + du_scr[pl.ds(t, 1), lanes] * twice(bx_ref[row0 + t])
                states[t] = h.astype(bf16)
            e2 = lax.dot_general(split_hi_lo(ds), jnp.concatenate(states, axis=0), nt,
                                 preferred_element_type=f32)
            dc = dc + (e2[:SUB] + e2[SUB:])
            a = a_ref[:, glob]
            g = g_scr[:, glob]
            ga = ga_out[:, glob]
            lams, rs = [None] * SUB, [None] * SUB
            for t in reversed(order):
                lam = twice(cx_ref[row0 + t]) * ds_ref[pl.ds(row0 + t, 1), lanes] + g
                lams[t] = lam.astype(bf16)
                g = decay[t] * lam
                r = g * prev[t] * a
                rs[t] = r.astype(bf16)
                ga = ga + dx_scr[pl.ds(t, 1), lanes] * r
            g_scr[:, glob] = g
            ga_out[:, glob] = ga
            lams = jnp.concatenate(lams, axis=0)
            s2 = jnp.dot(b2, lams, preferred_element_type=f32)
            s1 = s2[:SUB] + s2[SUB:]
            dd = jnp.dot(ones, jnp.concatenate(rs, axis=0), preferred_element_type=f32) + u * s1
            du_out[rows, lanes] = skip_ref[:, glob] * ds + delta * s1
            small = delta * (1.0 - delta * (0.5 - delta * (1.0 / 6.0)))
            sig = jnp.where(delta < 0.03, small, 1.0 - jnp.exp(-delta))
            dr = dd * sig
            dr_out[rows, lanes] = dr.astype(bf16)
            gb_out[:, glob] += dr
            gs_out[:, glob] += ds * u
            d2 = lax.dot_general(split_hi_lo(d_in), lams, nt, preferred_element_type=f32)
            db = db + (d2[:SUB] + d2[SUB:])
        db_out[rows, :] += fold(db)
        dc_out[rows, :] += fold(dc)
        return carry

    lax.fori_loop(0, subs, sub_step, 0)


def lane_groups(width_all, widths):
    for width in widths:
        if width_all % width == 0:
            return width
    return width_all


def scan_calls(rows, length, inner, backwards, tblock=128, width=None):
    width = width or lane_groups(inner, (1536, 1024, 512, 256))
    n_t, n_e, subs = length // tblock, inner // width, tblock // SUB
    params = pltpu.CompilerParams(dimension_semantics=("arbitrary",) * 3)

    def specs(flip):
        tb = (lambda i: n_t - 1 - i) if flip else (lambda i: i)
        tok = pl.BlockSpec((None, tblock, width), lambda r, i, e: (r, tb(i), e))
        lane = pl.BlockSpec((None, tblock, LANES), lambda r, i, e: (r, tb(i), 0))
        exp = pl.BlockSpec((None, tblock, NST, LANES), lambda r, i, e: (r, tb(i), 0, 0))
        til = pl.BlockSpec((None, tblock, SUB * NST), lambda r, i, e: (r, tb(i), 0))
        ck = pl.BlockSpec((None, subs, NST, width), lambda r, i, e: (r, tb(i), 0, e))
        full = pl.BlockSpec((NST, inner), lambda r, i, e: (0, 0))
        one = pl.BlockSpec((1, inner), lambda r, i, e: (0, 0))
        return tok, lane, exp, til, ck, full, one

    sds = jax.ShapeDtypeStruct
    tok, lane, exp, til, ck, full, one = specs(backwards)
    fwd = pl.pallas_call(
        functools.partial(fwd_kernel, backwards=backwards, subs=subs, width=width),
        grid=(rows, n_t, n_e),
        in_specs=[tok, tok, lane, exp, til, full, one],
        out_specs=[tok, ck],
        out_shape=[sds((rows, length, inner), f32), sds((rows, length // SUB, NST, inner), f32)],
        scratch_shapes=[pltpu.VMEM((NST, inner), f32)] + [pltpu.VMEM((SUB, width), f32)] * 2,
        compiler_params=params,
        name="scan_ahead_" + ("b" if backwards else "f"),
    )
    tok, lane, exp, til, ck, full, one = specs(not backwards)
    bwd = pl.pallas_call(
        functools.partial(bwd_kernel, backwards=backwards, subs=subs, width=width),
        grid=(rows, n_t, n_e),
        in_specs=[tok, tok, lane, exp, exp, til, tok, ck, full, full, one],
        out_specs=[tok, tok, lane, lane, full, full, full],
        out_shape=[sds((rows, length, inner), f32), sds((rows, length, inner), bf16),
                   sds((rows, length, LANES), f32), sds((rows, length, LANES), f32),
                   sds((NST, inner), f32), sds((SUB, inner), f32), sds((SUB, inner), f32)],
        scratch_shapes=[pltpu.VMEM((NST, inner), f32)] + [pltpu.VMEM((SUB, width), f32)] * 2,
        compiler_params=params,
        name="scan_back_" + ("b" if backwards else "f"),
    )
    return fwd, bwd


def conv_taps(pad_ref, row0, count, sign, masks_ref, lag):
    if lag == 0:
        return pad_ref[pl.ds(row0 + 8, count), :]
    side = 0 if sign > 0 else KCONV - 1
    return pad_ref[pl.ds(row0 + 8 - sign * lag, count), :] * masks_ref[side + lag - 1, pl.ds(row0, count), :]


def fill_padded(pad_ref, length):
    edge = jnp.zeros((8, LANES), f32)
    pad_ref[pl.ds(0, 8), :] = edge
    pad_ref[pl.ds(8 + length, 8), :] = edge


def conv_kernel(x_ref, masks_ref, w_ref, b_ref, u0_ref, u1_ref, pad_scr, *, length, chunk, tiles):
    for tile in range(tiles):
        lanes = pl.ds(tile * LANES, LANES)
        fill_padded(pad_scr, length)
        pad_scr[pl.ds(8, length), :] = x_ref[:, lanes]
        for row0 in range(0, length, chunk):
            for d, (sign, out) in enumerate(((1, u0_ref), (-1, u1_ref))):
                pre = b_ref[d:d + 1, lanes]
                for lag in range(KCONV):
                    tap = conv_taps(pad_scr, row0, chunk, sign, masks_ref, lag)
                    pre = pre + w_ref[d, lag:lag + 1, lanes] * tap
                out[pl.ds(row0, chunk), lanes] = (pre * jax.nn.sigmoid(pre)).astype(bf16)


def conv_back_kernel(x_ref, du0_ref, du1_ref, masks_ref, w_ref, b_ref, dx_ref, gw_ref, gb_ref,
                     pad_scr, dp0_scr, dp1_scr, *, length, chunk, tiles):
    both = ((1, du0_ref, dp0_scr), (-1, du1_ref, dp1_scr))
    for tile in range(tiles):
        lanes = pl.ds(tile * LANES, LANES)
        for ref in (pad_scr, dp0_scr, dp1_scr):
            fill_padded(ref, length)
        pad_scr[pl.ds(8, length), :] = x_ref[:, lanes]
        for d, (sign, du_ref, dp_scr) in enumerate(both):
            sums = [jnp.zeros((8, LANES), f32) for _ in range(KCONV + 1)]
            for row0 in range(0, length, chunk):
                taps = [conv_taps(pad_scr, row0, chunk, sign, masks_ref, lag) for lag in range(KCONV)]
                pre = b_ref[d:d + 1, lanes]
                for lag in range(KCONV):
                    pre = pre + w_ref[d, lag:lag + 1, lanes] * taps[lag]
                sg = jax.nn.sigmoid(pre)
                d_pre = du_ref[pl.ds(row0, chunk), lanes] * (sg * (1.0 + pre * (1.0 - sg)))
                dp_scr[pl.ds(row0 + 8, chunk), :] = d_pre
                for lag in range(KCONV + 1):
                    term = d_pre * taps[lag] if lag < KCONV else d_pre
                    sums[lag] = sums[lag] + jnp.sum(term.reshape(chunk // 8, 8, LANES), axis=0)
            for lag in range(KCONV):
                gw_ref[d, lag:lag + 1, lanes] = jnp.sum(sums[lag], axis=0, keepdims=True)
            gb_ref[d:d + 1, lanes] = jnp.sum(sums[KCONV], axis=0, keepdims=True)
        for row0 in range(0, length, chunk):
            total = jnp.zeros((chunk, LANES), f32)
            for d, (sign, _, dp_scr) in enumerate(both):
                for lag in range(KCONV):
                    total = total + w_ref[d, lag:lag + 1, lanes] * conv_taps(
                        dp_scr, row0, chunk, -sign, masks_ref, lag)
            dx_ref[pl.ds(row0, chunk), lanes] = total.astype(bf16)


def conv_calls(length, inner, width=256, chunk=64):
    if inner % width:
        width = LANES
    tok = pl.BlockSpec((length, width), lambda e: (0, e))
    masks = pl.BlockSpec((2 * (KCONV - 1), length, LANES), lambda e: (0, 0, 0))
    taps = pl.BlockSpec((2, KCONV, width), lambda e: (0, 0, e))
    bias = pl.BlockSpec((2, width), lambda e: (0, e))
    sds = jax.ShapeDtypeStruct
    pad = pltpu.VMEM((length + 16, LANES), f32)
    sizes = dict(length=length, chunk=chunk, tiles=width // LANES)
    params = pltpu.CompilerParams(dimension_semantics=("arbitrary",))
    ahead = pl.pallas_call(
        functools.partial(conv_kernel, **sizes), grid=(inner // width,),
        in_specs=[tok, masks, taps, bias], out_specs=[tok, tok],
        out_shape=[sds((length, inner), bf16)] * 2, scratch_shapes=[pad],
        compiler_params=params, name="conv_ahead")
    back = pl.pallas_call(
        functools.partial(conv_back_kernel, **sizes), grid=(inner // width,),
        in_specs=[tok, tok, tok, masks, taps, bias], out_specs=[tok, taps, bias],
        out_shape=[sds((length, inner), bf16), sds((2, KCONV, inner), f32), sds((2, inner), f32)],
        scratch_shapes=[pad] * 3, compiler_params=params, name="conv_back")
    return ahead, back


EPS = 1e-06
AXES = ("dp", "fsdp")
BIG = 1e30
LOG2E = 1.4426950408889634


def mm(a, b, dims):
    return lax.dot_general(a, b, (dims, ((), ())), preferred_element_type=f32)


def to_all(v):
    owners = lax.axis_size(AXES)
    return lax.all_to_all(jnp.broadcast_to(v[None], (owners,) + v.shape), AXES, 0, 0, tiled=True)


def gather0(v):
    return lax.all_gather(v, AXES, axis=0, tiled=True)


def scatter0(v):
    return lax.psum_scatter(v, AXES, scatter_dimension=0, tiled=True)


def tied(v, *after):
    return lax.optimization_barrier((v,) + after)[0]


def item_masks(ids):
    length = ids.shape[0]
    pad = jnp.full((KCONV - 1,), -1, ids.dtype)
    long = jnp.concatenate([pad, ids, pad])
    shifts = [-lag for lag in range(1, KCONV)] + list(range(1, KCONV))
    rows = [(long[KCONV - 1 + s:KCONV - 1 + s + length] == ids).astype(f32) for s in shifts]
    return jnp.broadcast_to(jnp.stack(rows)[:, :, None], (len(rows), length, LANES))


def body(tokens_in, condition, item_flags, grad_out, in_weight, out_weight, x_projection,
         dt_projection, conv_weight, conv_bias, dt_bias, decay_log, skip_gain, mod_weight, mod_bias):
    length, model = tokens_in.shape[1:]
    owners = lax.axis_size(AXES)
    me = lax.axis_index(AXES)
    inner = in_weight.shape[1] // 2
    own_model = in_weight.shape[0]
    rank = dt_projection.shape[1]

    own_inner = out_weight.shape[0]
    side = jnp.pad(jnp.swapaxes(dt_projection, 1, 2), ((0, 0), (0, 0), (0, LANES - rank)))
    pair = jnp.stack([x_projection, side])
    first = gather0(jnp.concatenate([in_weight[:, :inner], pair.reshape(-1, inner)], axis=0))
    first = first.reshape(owners, -1, inner)
    w_x = first[:, :own_model].reshape(-1, inner)
    pair = jnp.moveaxis(first[:, own_model:].reshape(owners, 2, 2, own_inner, LANES), 0, 2)
    w_xp, w_dt = pair.reshape(2, 2, inner, LANES)
    w_z = gather0(in_weight[:, inner:])
    w_o = gather0(out_weight)

    cond = condition[0].astype(f32)
    act = jax.nn.silu(cond).astype(bf16)
    smalls = (act, conv_weight, conv_bias, dt_bias, decay_log, skip_gain, mod_bias)
    flat = jnp.concatenate([v.reshape(-1) for v in smalls])
    flat = jnp.pad(flat, (0, -flat.shape[0] % (8 * LANES)))
    everyone = to_all(flat.reshape(-1, LANES)).reshape(owners, -1)
    parts, at = [], 0
    for v in smalls:
        parts.append(everyone[:, at:at + v.size].reshape((owners,) + v.shape))
        at += v.size
    act_all = parts[0].reshape(owners * 2, model)
    join = lambda v, dim: jnp.moveaxis(v, 0, dim).reshape(
        v.shape[1:dim + 1] + (owners * v.shape[dim + 1],) + v.shape[dim + 2:]).astype(f32)
    conv_w, conv_b, dt_b = join(parts[1], 2), join(parts[2], 1), join(parts[3], 1)
    log_rate, skip = join(parts[4], 1), join(parts[5], 1)
    modb = parts[6].reshape(-1).astype(f32)

    act_own = lax.dynamic_slice(act_all, (0, me * own_model), (owners * 2, own_model))
    partial = mm(act_own, mod_weight, ((1,), (0,))).reshape(owners, 2, -1)
    mods = jnp.sum(lax.all_to_all(partial, AXES, 0, 0, tiled=True), axis=0) + modb

    flags = item_flags[0]
    ids = jnp.cumsum(flags, dtype=jnp.int32) - 1
    second = (ids == 1)[:, None]
    pick = lambda v: jnp.where(second, v[1], v[0])
    shift, scale, gate = (mods[:, i * model:(i + 1) * model] for i in range(3))
    masks = item_masks(ids)

    x = tokens_in[0].astype(f32)
    mean = jnp.mean(x, axis=1, keepdims=True)
    centered = x - mean
    inv = lax.rsqrt(jnp.mean(centered * centered, axis=1, keepdims=True) + EPS)
    normed = centered * inv
    hidden = (normed * (1.0 + pick(scale)) + pick(shift)).astype(bf16)
    xs = mm(hidden, w_x, ((1,), (0,)))

    g = grad_out[0].astype(f32)
    d_branch = (g * pick(gate)).astype(bf16)

    starts = flags.astype(f32)
    starts_b = jnp.concatenate([starts[1:], jnp.ones((1,), f32)])
    calls = [scan_calls(1, length, inner, bool(d)) for d in range(2)]
    conv_ahead, conv_back = conv_calls(length, inner)
    wide = lambda v: jnp.broadcast_to(v[None, :, :, None], (1, length, NST, LANES))
    tile = lambda v: jnp.tile(v, (1, SUB))[None]
    us = conv_ahead(xs, masks, conv_w, conv_b)
    kept = []
    for d in range(2):
        u = us[d]
        proj = mm(u, w_xp[d], ((1,), (0,)))
        dt_low = proj.astype(bf16)
        b_m, c_m = proj[:, rank:rank + NST], proj[:, rank + NST:]
        delta = jax.nn.softplus(mm(dt_low, w_dt[d], ((1,), (1,))) + dt_b[d])
        rate = -jnp.exp(log_rate[d]).T
        rate2 = rate * LOG2E
        sb = jnp.broadcast_to((BIG * (starts_b if d else starts))[None, :, None], (1, length, LANES))
        b_wide = wide(b_m)
        y, ck = calls[d][0](delta[None], u[None], sb, b_wide, tile(c_m), rate2, skip[d][None])
        kept.append((u, dt_low, b_m, c_m, delta, rate, rate2, sb, b_wide, y[0], ck))
    both = kept[0][9] + kept[1][9]
    z = mm(tied(hidden, both), w_z, ((1,), (0,)))
    sig_z = jax.nn.sigmoid(z)
    silu_z = z * sig_z
    gated = (both * silu_z).astype(bf16)
    grad_out_w = mm(gated, d_branch, ((0,), (0,))).astype(bf16)

    d_gated = mm(d_branch, w_o, ((1,), (1,)))
    d_scan = d_gated * silu_z
    d_z = (d_gated * both * sig_z * (1.0 + z * (1.0 - sig_z))).astype(bf16)
    grad_in_z = mm(hidden, d_z, ((0,), (0,))).astype(bf16)
    d_scan, grad_out_w, grad_in_z = lax.optimization_barrier((d_scan, grad_out_w, grad_in_z))
    grad_out_w = scatter0(grad_out_w)
    grad_in_z = scatter0(grad_in_z)
    branch = mm(gated, w_o, ((1,), (0,)))
    block_out = (x + pick(gate) * branch).astype(bf16)
    d_gate = g * branch
    lane = lax.broadcasted_iota(jnp.int32, (1, LANES), 1)
    d_us, g_xps, g_dts, g_dbs, g_als, g_sks = [], [], [], [], [], []
    for d in range(2):
        u, dt_low, b_m, c_m, delta, rate, rate2, sb, b_wide, _, ck = kept[d]
        du, dr, db, dc, ga, gs, gb = calls[d][1](
            delta[None], u[None], sb, b_wide, wide(c_m), tile(b_m), d_scan[None], ck, rate, rate2,
            skip[d][None])
        dr = dr[0]
        d_low = mm(dr, w_dt[d], ((1,), (0,)))
        d_proj = jnp.where(lane < rank, d_low, jnp.where(lane < rank + NST, db[0], dc[0])).astype(bf16)
        g_dts.append(mm(dr, dt_low, ((0,), (0,))))
        g_xps.append(mm(u, d_proj, ((0,), (0,))))
        d_us.append(du[0] + mm(d_proj, w_xp[d], ((1,), (1,))))
        g_dbs.append(jnp.sum(gb, axis=0))
        g_als.append(ga.T)
        g_sks.append(jnp.sum(gs, axis=0))
    d_xs, g_cw, g_cb = conv_back(xs, d_us[0], d_us[1], masks, conv_w, conv_b)
    grad_in_x = mm(hidden, d_xs, ((0,), (0,))).astype(bf16)

    wide_rows = [jnp.stack(v).astype(bf16).reshape(2, owners, own_inner, LANES) for v in (g_xps, g_dts)]
    wide_rows = jnp.concatenate([jnp.moveaxis(v, 1, 0).reshape(owners, -1, LANES) for v in wide_rows], axis=1)
    stacked = [g_cw, g_cb, jnp.stack(g_dbs), jnp.stack(g_als), jnp.stack(g_sks)]
    dims = (2, 1, 1, 1, 1)
    pieces, shapes = [], []
    for v, dim in zip(stacked, dims):
        shape = v.shape[:dim] + (owners, v.shape[dim] // owners) + v.shape[dim + 1:]
        pieces.append(jnp.moveaxis(v.reshape(shape), dim, 0).reshape(owners, -1).astype(bf16))
        shapes.append(v.shape[:dim] + (v.shape[dim] // owners,) + v.shape[dim + 1:])
    packed = jnp.concatenate(pieces, axis=1)
    packed = jnp.pad(packed, ((0, 0), (0, -packed.shape[1] % (16 * LANES))))
    packed = jnp.concatenate([wide_rows, packed.reshape(owners, -1, LANES)], axis=1)
    grad_in_x = scatter0(tied(grad_in_x, grad_in_z))
    received = lax.all_to_all(packed, AXES, 0, 0, tiled=True)
    mine = jnp.sum(received.astype(f32), axis=0)
    grad_in = jnp.concatenate([grad_in_x, grad_in_z], axis=1).astype(f32)
    both_rows = mine[:4 * own_inner].reshape(2, 2, own_inner, LANES)
    g_xp = both_rows[0]
    g_dt = jnp.swapaxes(both_rows[1][..., :rank], 1, 2)
    mine = mine[4 * own_inner:].reshape(-1)
    small_grads, at = [], 0
    for shape in shapes:
        count = 1
        for n in shape:
            count *= n
        small_grads.append(mine[at:at + count].reshape(shape))
        at += count

    d_hidden = mm(d_xs, w_x, ((1,), (1,))) + mm(d_z, w_z, ((1,), (1,)))
    scale_tok = 1.0 + pick(scale)
    d_n = d_hidden * scale_tok
    m1 = jnp.mean(d_n, axis=1, keepdims=True)
    m2 = jnp.mean(d_n * normed, axis=1, keepdims=True)
    grad_tokens = g + (d_n - m1 - normed * m2) * inv
    by_item = lambda v: jnp.stack([jnp.sum(jnp.where(second, 0.0, v), axis=0),
                                   jnp.sum(jnp.where(second, v, 0.0), axis=0)])
    d_mods = jnp.concatenate([by_item(d_hidden), by_item(d_hidden * normed), by_item(d_gate)], axis=1)
    d_mods_all = to_all(d_mods.astype(bf16)).reshape(owners * 2, -1)
    grad_mod_w = mm(act_own, d_mods_all, ((0,), (0,)))
    own_b = mod_bias.shape[0]
    grad_mod_b = jnp.sum(
        lax.dynamic_slice(d_mods_all, (0, me * own_b), (owners * 2, own_b)).astype(f32), axis=0)
    d_act = mm(d_mods_all, mod_weight, ((1,), (1,))).reshape(owners, 2, own_model)
    d_act = lax.all_to_all(d_act, AXES, 0, 0, tiled=True)
    d_act = jnp.moveaxis(d_act, 0, 1).reshape(2, model)
    sc = jax.nn.sigmoid(cond)
    grad_cond = d_act * sc * (1.0 + cond * (1.0 - sc))
    g_cw, g_cb, g_db, g_al, g_sk = small_grads
    return (block_out[None], grad_tokens[None], grad_cond[None], grad_in, grad_out_w.astype(f32), g_xp,
            g_dt, g_cw, g_cb, g_db, g_al, g_sk, grad_mod_w, grad_mod_b)


def solution(mesh):
    row3, row2, row1 = P(AXES, None, None), P(AXES, None), P(AXES)
    mid3, mid2, last3 = P(None, AXES, None), P(None, AXES), P(None, None, AXES)
    weights = (row2, row2, mid3, last3, last3, mid2, mid2, mid3, mid2, row2, row1)
    return jax.shard_map(
        body, mesh=mesh, in_specs=(row3, row3, row2, row3) + weights,
        out_specs=(row3, row3, row3) + weights, check_vma=False)
```

```python
import functools

import jax
import jax.numpy as jnp
from jax import lax
from jax.experimental import pallas as pl
from jax.experimental.pallas import tpu as pltpu
from jax.sharding import PartitionSpec as P

NST = 16
SUB = 16
KCONV = 4
LANES = 128
bf16 = jnp.bfloat16
f32 = jnp.float32


def split_hi_lo(v):
    hi = v.astype(bf16)
    lo = (v - hi.astype(f32)).astype(bf16)
    return jnp.concatenate([hi, lo], axis=0)


def block_diag(tiled):
    rows = lax.broadcasted_iota(jnp.int32, tiled.shape, 0)
    cols = lax.broadcasted_iota(jnp.int32, tiled.shape, 1) // NST
    return jnp.where(rows == cols, tiled, 0.0)


PAIR = 256


def fold(v):
    v = block_diag(v)
    v = v[:, :LANES] + v[:, LANES:]
    for by in (64, 32, 16):
        v = v + pltpu.roll(v, by, 1)
    return v


def fwd_kernel(delta_ref, u_ref, sb_ref, bx_ref, ct_ref, a2_ref, skip_ref, y_ref, ck_ref,
               h_scr, dx_scr, du_scr, *, backwards, subs, width):
    lane0 = pl.multiple_of(pl.program_id(2) * width, width)

    @pl.when(pl.program_id(1) == 0)
    def _():
        h_scr[:, pl.ds(lane0, width)] = jnp.zeros((NST, width), f32)

    order = range(SUB - 1, -1, -1) if backwards else range(SUB)

    def sub_step(step, carry):
        sub = subs - 1 - step if backwards else step
        row0 = pl.multiple_of(sub * SUB, SUB)
        rows = pl.ds(row0, SUB)
        sb = sb_ref[rows, :]
        sb = jnp.concatenate([sb] * (PAIR // LANES), axis=1)
        c2 = split_hi_lo(block_diag(ct_ref[rows, :]))
        for p in range(width // PAIR):
            lanes = pl.ds(p * PAIR, PAIR)
            glob = pl.ds(lane0 + p * PAIR, PAIR)
            delta = delta_ref[rows, lanes]
            u = u_ref[rows, lanes].astype(f32)
            du_scr[:, lanes] = delta * u
            dx_scr[:, lanes] = delta + sb
            h = h_scr[:, glob]
            a2 = a2_ref[:, glob]
            ck_ref[sub, :, lanes] = h
            states = [None] * SUB
            for t in order:
                b = bx_ref[row0 + t]
                b = jnp.concatenate([b] * (PAIR // LANES), axis=1)
                h = jnp.exp2(dx_scr[pl.ds(t, 1), lanes] * a2) * h + du_scr[pl.ds(t, 1), lanes] * b
                states[t] = h.astype(bf16)
            h_scr[:, glob] = h
            y2 = jnp.dot(c2, jnp.concatenate(states, axis=0), preferred_element_type=f32)
            y_ref[rows, lanes] = y2[:SUB] + y2[SUB:] + skip_ref[:, glob] * u
        return carry

    lax.fori_loop(0, subs, sub_step, 0)


def bwd_kernel(delta_ref, u_ref, sb_ref, bx_ref, cx_ref, bt_ref, ds_ref, ck_ref, a_ref, a2_ref,
               skip_ref, du_out, dr_out, db_out, dc_out, ga_out, gs_out, gb_out,
               g_scr, dx_scr, du_scr, *, backwards, subs, width):
    first = pl.program_id(1) == 0
    start = jnp.logical_and(first, pl.program_id(0) == 0)
    eg = pl.program_id(2)
    lane0 = pl.multiple_of(eg * width, width)
    wide = pl.ds(lane0, width)

    @pl.when(first)
    def _():
        g_scr[:, wide] = jnp.zeros((NST, width), f32)

    @pl.when(start)
    def _():
        ga_out[:, wide] = jnp.zeros((NST, width), f32)
        gs_out[:, wide] = jnp.zeros((SUB, width), f32)
        gb_out[:, wide] = jnp.zeros((SUB, width), f32)

    @pl.when(eg == 0)
    def _():
        db_out[...] = jnp.zeros_like(db_out)
        dc_out[...] = jnp.zeros_like(dc_out)

    order = list(range(SUB - 1, -1, -1) if backwards else range(SUB))
    nt = (((1,), (1,)), ((), ()))
    twice = lambda v: jnp.concatenate([v] * (PAIR // LANES), axis=1)

    def sub_step(step, carry):
        sub = step if backwards else subs - 1 - step
        row0 = pl.multiple_of(sub * SUB, SUB)
        rows = pl.ds(row0, SUB)
        sb = twice(sb_ref[rows, :])
        b2 = split_hi_lo(block_diag(bt_ref[rows, :]))
        ones = block_diag(jnp.ones((SUB, SUB * NST), f32)).astype(bf16)
        db, dc = jnp.zeros((SUB, SUB * NST), f32), jnp.zeros((SUB, SUB * NST), f32)
        for p in range(width // PAIR):
            lanes = pl.ds(p * PAIR, PAIR)
            glob = pl.ds(lane0 + p * PAIR, PAIR)
            delta = delta_ref[rows, lanes]
            u = u_ref[rows, lanes].astype(f32)
            ds = ds_ref[rows, lanes]
            d_in = delta * u
            du_scr[:, lanes] = d_in
            dx_scr[:, lanes] = delta + sb
            a2 = a2_ref[:, glob]
            h = ck_ref[sub, :, lanes]
            prev, decay, states = [None] * SUB, [None] * SUB, [None] * SUB
            for t in order:
                prev[t] = h
                decay[t] = jnp.exp2(dx_scr[pl.ds(t, 1), lanes] * a2)
                h = decay[t] * h + du_scr[pl.ds(t, 1), lanes] * twice(bx_ref[row0 + t])
                states[t] = h.astype(bf16)
            e2 = lax.dot_general(split_hi_lo(ds), jnp.concatenate(states, axis=0), nt,
                                 preferred_element_type=f32)
            dc = dc + (e2[:SUB] + e2[SUB:])
            a = a_ref[:, glob]
            g = g_scr[:, glob]
            ga = ga_out[:, glob]
            lams, rs = [None] * SUB, [None] * SUB
            for t in reversed(order):
                lam = twice(cx_ref[row0 + t]) * ds_ref[pl.ds(row0 + t, 1), lanes] + g
                lams[t] = lam.astype(bf16)
                g = decay[t] * lam
                r = g * prev[t] * a
                rs[t] = r.astype(bf16)
                ga = ga + dx_scr[pl.ds(t, 1), lanes] * r
            g_scr[:, glob] = g
            ga_out[:, glob] = ga
            lams = jnp.concatenate(lams, axis=0)
            s2 = jnp.dot(b2, lams, preferred_element_type=f32)
            s1 = s2[:SUB] + s2[SUB:]
            dd = jnp.dot(ones, jnp.concatenate(rs, axis=0), preferred_element_type=f32) + u * s1
            du_out[rows, lanes] = skip_ref[:, glob] * ds + delta * s1
            small = delta * (1.0 - delta * (0.5 - delta * (1.0 / 6.0)))
            sig = jnp.where(delta < 0.03, small, 1.0 - jnp.exp(-delta))
            dr = dd * sig
            dr_out[rows, lanes] = dr.astype(bf16)
            gb_out[:, glob] += dr
            gs_out[:, glob] += ds * u
            d2 = lax.dot_general(split_hi_lo(d_in), lams, nt, preferred_element_type=f32)
            db = db + (d2[:SUB] + d2[SUB:])
        db_out[rows, :] += fold(db)
        dc_out[rows, :] += fold(dc)
        return carry

    lax.fori_loop(0, subs, sub_step, 0)


def lane_groups(width_all, widths):
    for width in widths:
        if width_all % width == 0:
            return width
    return width_all


def scan_calls(rows, length, inner, backwards, tblock=128, width=None):
    width = width or lane_groups(inner, (1536, 1024, 512, 256))
    n_t, n_e, subs = length // tblock, inner // width, tblock // SUB
    params = pltpu.CompilerParams(dimension_semantics=("arbitrary",) * 3)

    def specs(flip):
        tb = (lambda i: n_t - 1 - i) if flip else (lambda i: i)
        tok = pl.BlockSpec((None, tblock, width), lambda r, i, e: (r, tb(i), e))
        lane = pl.BlockSpec((None, tblock, LANES), lambda r, i, e: (r, tb(i), 0))
        exp = pl.BlockSpec((None, tblock, NST, LANES), lambda r, i, e: (r, tb(i), 0, 0))
        til = pl.BlockSpec((None, tblock, SUB * NST), lambda r, i, e: (r, tb(i), 0))
        ck = pl.BlockSpec((None, subs, NST, width), lambda r, i, e: (r, tb(i), 0, e))
        full = pl.BlockSpec((NST, inner), lambda r, i, e: (0, 0))
        one = pl.BlockSpec((1, inner), lambda r, i, e: (0, 0))
        return tok, lane, exp, til, ck, full, one

    sds = jax.ShapeDtypeStruct
    tok, lane, exp, til, ck, full, one = specs(backwards)
    fwd = pl.pallas_call(
        functools.partial(fwd_kernel, backwards=backwards, subs=subs, width=width),
        grid=(rows, n_t, n_e),
        in_specs=[tok, tok, lane, exp, til, full, one],
        out_specs=[tok, ck],
        out_shape=[sds((rows, length, inner), f32), sds((rows, length // SUB, NST, inner), f32)],
        scratch_shapes=[pltpu.VMEM((NST, inner), f32)] + [pltpu.VMEM((SUB, width), f32)] * 2,
        compiler_params=params,
        name="scan_ahead_" + ("b" if backwards else "f"),
    )
    tok, lane, exp, til, ck, full, one = specs(not backwards)
    bwd = pl.pallas_call(
        functools.partial(bwd_kernel, backwards=backwards, subs=subs, width=width),
        grid=(rows, n_t, n_e),
        in_specs=[tok, tok, lane, exp, exp, til, tok, ck, full, full, one],
        out_specs=[tok, tok, lane, lane, full, full, full],
        out_shape=[sds((rows, length, inner), f32), sds((rows, length, inner), bf16),
                   sds((rows, length, LANES), f32), sds((rows, length, LANES), f32),
                   sds((NST, inner), f32), sds((SUB, inner), f32), sds((SUB, inner), f32)],
        scratch_shapes=[pltpu.VMEM((NST, inner), f32)] + [pltpu.VMEM((SUB, width), f32)] * 2,
        compiler_params=params,
        name="scan_back_" + ("b" if backwards else "f"),
    )
    return fwd, bwd


def conv_taps(pad_ref, row0, count, sign, masks_ref, lag):
    if lag == 0:
        return pad_ref[pl.ds(row0 + 8, count), :]
    side = 0 if sign > 0 else KCONV - 1
    return pad_ref[pl.ds(row0 + 8 - sign * lag, count), :] * masks_ref[side + lag - 1, pl.ds(row0, count), :]


def fill_padded(pad_ref, length):
    edge = jnp.zeros((8, LANES), f32)
    pad_ref[pl.ds(0, 8), :] = edge
    pad_ref[pl.ds(8 + length, 8), :] = edge


def project_conv_kernel(h_ref, wts_ref, masks_ref, w_ref, b_ref, x_ref, u0_ref, u1_ref, pad_scr,
                        *, length, chunk, width):
    for half in range(width // PAIR):
        cols = pl.ds(half * PAIR, PAIR)
        wts = wts_ref[:, :, cols].reshape(h_ref.shape[1], PAIR)
        x_ref[:, cols] = jnp.dot(h_ref[...], wts, preferred_element_type=f32)
    for tile in range(width // LANES):
        lanes = pl.ds(tile * LANES, LANES)
        pad = pad_scr.at[tile % 2]
        fill_padded(pad, length)
        pad[pl.ds(8, length), :] = x_ref[:, lanes]
        for row0 in range(0, length, chunk):
            for d, (sign, out) in enumerate(((1, u0_ref), (-1, u1_ref))):
                pre = b_ref[d:d + 1, lanes]
                for lag in range(KCONV):
                    tap = conv_taps(pad, row0, chunk, sign, masks_ref, lag)
                    pre = pre + w_ref[d, lag:lag + 1, lanes] * tap
                out[pl.ds(row0, chunk), lanes] = (pre * jax.nn.sigmoid(pre)).astype(bf16)


def back_project_kernel(dx_ref, dz_ref, wx_ref, wz_ref, out_ref, *, width):
    @pl.when(pl.program_id(0) == 0)
    def _():
        out_ref[...] = jnp.zeros_like(out_ref)

    nt = (((1,), (1,)), ((), ()))
    wx = wx_ref[...].reshape(out_ref.shape[1], width)
    out_ref[...] += (lax.dot_general(dx_ref[...], wx, nt, preferred_element_type=f32)
                     + lax.dot_general(dz_ref[...], wz_ref[...], nt, preferred_element_type=f32))


def conv_back_kernel(x_ref, du0_ref, du1_ref, masks_ref, w_ref, b_ref, dx_ref, gw_ref, gb_ref,
                     pad_scr, dp0_scr, dp1_scr, *, length, chunk, tiles):
    both = ((1, du0_ref, dp0_scr), (-1, du1_ref, dp1_scr))
    for tile in range(tiles):
        lanes = pl.ds(tile * LANES, LANES)
        for ref in (pad_scr, dp0_scr, dp1_scr):
            fill_padded(ref, length)
        pad_scr[pl.ds(8, length), :] = x_ref[:, lanes]
        for d, (sign, du_ref, dp_scr) in enumerate(both):
            sums = [jnp.zeros((8, LANES), f32) for _ in range(KCONV + 1)]
            for row0 in range(0, length, chunk):
                taps = [conv_taps(pad_scr, row0, chunk, sign, masks_ref, lag) for lag in range(KCONV)]
                pre = b_ref[d:d + 1, lanes]
                for lag in range(KCONV):
                    pre = pre + w_ref[d, lag:lag + 1, lanes] * taps[lag]
                sg = jax.nn.sigmoid(pre)
                d_pre = du_ref[pl.ds(row0, chunk), lanes] * (sg * (1.0 + pre * (1.0 - sg)))
                dp_scr[pl.ds(row0 + 8, chunk), :] = d_pre
                for lag in range(KCONV + 1):
                    term = d_pre * taps[lag] if lag < KCONV else d_pre
                    sums[lag] = sums[lag] + jnp.sum(term.reshape(chunk // 8, 8, LANES), axis=0)
            for lag in range(KCONV):
                gw_ref[d, lag:lag + 1, lanes] = jnp.sum(sums[lag], axis=0, keepdims=True)
            gb_ref[d:d + 1, lanes] = jnp.sum(sums[KCONV], axis=0, keepdims=True)
        for row0 in range(0, length, chunk):
            total = jnp.zeros((chunk, LANES), f32)
            for d, (sign, _, dp_scr) in enumerate(both):
                for lag in range(KCONV):
                    total = total + w_ref[d, lag:lag + 1, lanes] * conv_taps(
                        dp_scr, row0, chunk, -sign, masks_ref, lag)
            dx_ref[pl.ds(row0, chunk), lanes] = total.astype(bf16)


def gate_kernel(h_ref, g_ref, wz_ref, wo_ref, y0_ref, y1_ref, gated_ref, ds_ref, dz_ref, z_scr, d_scr,
                *, length, chunk):
    z_scr[...] = jnp.dot(h_ref[...], wz_ref[...], preferred_element_type=f32)
    d_scr[...] = lax.dot_general(g_ref[...], wo_ref[...], (((1,), (1,)), ((), ())),
                                 preferred_element_type=f32)
    for row0 in range(0, length, chunk):
        rows = pl.ds(row0, chunk)
        z, d_gated = z_scr[rows, :], d_scr[rows, :]
        both = y0_ref[rows, :] + y1_ref[rows, :]
        sig = jax.nn.sigmoid(z)
        silu = z * sig
        gated_ref[rows, :] = (both * silu).astype(bf16)
        ds_ref[rows, :] = d_gated * silu
        dz_ref[rows, :] = (d_gated * both * sig * (1.0 + z * (1.0 - sig))).astype(bf16)


def gate_call(length, model, inner, width=384, chunk=32):
    if inner % width:
        width = PAIR
    tok = pl.BlockSpec((length, width), lambda e: (0, e))
    every = pl.BlockSpec((length, model), lambda e: (0, 0))
    sds = jax.ShapeDtypeStruct
    return pl.pallas_call(
        functools.partial(gate_kernel, length=length, chunk=chunk), grid=(inner // width,),
        in_specs=[every, every, pl.BlockSpec((model, width), lambda e: (0, e)),
                  pl.BlockSpec((width, model), lambda e: (e, 0)), tok, tok],
        out_specs=[tok, tok, tok],
        out_shape=[sds((length, inner), bf16), sds((length, inner), f32), sds((length, inner), bf16)],
        scratch_shapes=[pltpu.VMEM((length, width), f32)] * 2,
        compiler_params=pltpu.CompilerParams(dimension_semantics=("arbitrary",)), name="gate")


def projection_calls(length, model, inner, blocks, width=512, chunk=64):
    if inner % width:
        width = PAIR
    rows = model // blocks
    tok = pl.BlockSpec((length, width), lambda e: (0, e))
    every = pl.BlockSpec((length, model), lambda e: (0, 0))
    wts = pl.BlockSpec((blocks, rows, width), lambda e: (0, 0, e))
    flat = pl.BlockSpec((model, width), lambda e: (0, e))
    masks = pl.BlockSpec((2 * (KCONV - 1), length, LANES), lambda e: (0, 0, 0))
    taps = pl.BlockSpec((2, KCONV, width), lambda e: (0, 0, e))
    bias = pl.BlockSpec((2, width), lambda e: (0, e))
    sds = jax.ShapeDtypeStruct
    params = pltpu.CompilerParams(dimension_semantics=("arbitrary",))
    ahead = pl.pallas_call(
        functools.partial(project_conv_kernel, length=length, chunk=chunk, width=width),
        grid=(inner // width,), in_specs=[every, wts, masks, taps, bias], out_specs=[tok, tok, tok],
        out_shape=[sds((length, inner), f32)] + [sds((length, inner), bf16)] * 2,
        scratch_shapes=[pltpu.VMEM((2, length + 16, LANES), f32)], compiler_params=params,
        name="project_conv")
    back = pl.pallas_call(
        functools.partial(back_project_kernel, width=width), grid=(inner // width,),
        in_specs=[tok, tok, wts, flat], out_specs=every,
        out_shape=sds((length, model), f32), compiler_params=params, name="back_project")
    return ahead, back


def conv_back_call(length, inner, width=256, chunk=64):
    if inner % width:
        width = LANES
    tok = pl.BlockSpec((length, width), lambda e: (0, e))
    masks = pl.BlockSpec((2 * (KCONV - 1), length, LANES), lambda e: (0, 0, 0))
    taps = pl.BlockSpec((2, KCONV, width), lambda e: (0, 0, e))
    bias = pl.BlockSpec((2, width), lambda e: (0, e))
    sds = jax.ShapeDtypeStruct
    pad = pltpu.VMEM((length + 16, LANES), f32)
    sizes = dict(length=length, chunk=chunk, tiles=width // LANES)
    params = pltpu.CompilerParams(dimension_semantics=("arbitrary",))
    back = pl.pallas_call(
        functools.partial(conv_back_kernel, **sizes), grid=(inner // width,),
        in_specs=[tok, tok, tok, masks, taps, bias], out_specs=[tok, taps, bias],
        out_shape=[sds((length, inner), bf16), sds((2, KCONV, inner), f32), sds((2, inner), f32)],
        scratch_shapes=[pad] * 3, compiler_params=params, name="conv_back")
    return back


EPS = 1e-06
AXES = ("dp", "fsdp")
BIG = 1e30
LOG2E = 1.4426950408889634


def mm(a, b, dims):
    return lax.dot_general(a, b, (dims, ((), ())), preferred_element_type=f32)


def to_all(v):
    owners = lax.axis_size(AXES)
    return lax.all_to_all(jnp.broadcast_to(v[None], (owners,) + v.shape), AXES, 0, 0, tiled=True)


def gather0(v):
    return lax.all_gather(v, AXES, axis=0, tiled=True)


def tied(v, *after):
    return lax.optimization_barrier((v,) + after)[0]


def item_masks(ids):
    length = ids.shape[0]
    pad = jnp.full((KCONV - 1,), -1, ids.dtype)
    long = jnp.concatenate([pad, ids, pad])
    shifts = [-lag for lag in range(1, KCONV)] + list(range(1, KCONV))
    rows = [(long[KCONV - 1 + s:KCONV - 1 + s + length] == ids).astype(f32) for s in shifts]
    return jnp.broadcast_to(jnp.stack(rows)[:, :, None], (len(rows), length, LANES))


def body(tokens_in, condition, item_flags, grad_out, in_weight, out_weight, x_projection,
         dt_projection, conv_weight, conv_bias, dt_bias, decay_log, skip_gain, mod_weight, mod_bias):
    length, model = tokens_in.shape[1:]
    owners = lax.axis_size(AXES)
    me = lax.axis_index(AXES)
    inner = in_weight.shape[1] // 2
    own_model = in_weight.shape[0]
    rank = dt_projection.shape[1]

    own_inner = out_weight.shape[0]
    side = jnp.pad(jnp.swapaxes(dt_projection, 1, 2), ((0, 0), (0, 0), (0, LANES - rank)))
    pair = jnp.stack([x_projection, side])
    first = gather0(jnp.concatenate([in_weight[:, :inner], pair.reshape(-1, inner)], axis=0))

    cond = condition[0].astype(f32)
    act = jax.nn.silu(cond).astype(bf16)
    smalls = (act, conv_weight, conv_bias, dt_bias, decay_log, skip_gain, mod_bias)
    flat = jnp.concatenate([v.reshape(-1) for v in smalls])
    flat = jnp.pad(flat, (0, -flat.shape[0] % (8 * LANES)))
    everyone = to_all(flat.reshape(-1, LANES)).reshape(owners, -1)
    parts, at = [], 0
    for v in smalls:
        parts.append(everyone[:, at:at + v.size].reshape((owners,) + v.shape))
        at += v.size
    act_all = parts[0].reshape(owners * 2, model)
    join = lambda v, dim: jnp.moveaxis(v, 0, dim).reshape(
        v.shape[1:dim + 1] + (owners * v.shape[dim + 1],) + v.shape[dim + 2:]).astype(f32)
    conv_w, conv_b, dt_b = join(parts[1], 2), join(parts[2], 1), join(parts[3], 1)
    log_rate, skip = join(parts[4], 1), join(parts[5], 1)
    modb = parts[6].reshape(-1).astype(f32)

    act_own = lax.dynamic_slice(act_all, (0, me * own_model), (owners * 2, own_model))
    partial = mm(act_own, mod_weight, ((1,), (0,))).reshape(owners, 2, -1)
    mods = jnp.sum(lax.all_to_all(partial, AXES, 0, 0, tiled=True), axis=0) + modb
    flags = item_flags[0]
    ids = jnp.cumsum(flags, dtype=jnp.int32) - 1
    second = (ids == 1)[:, None]
    pick = lambda v: jnp.where(second, v[1], v[0])
    shift, scale, gate = (mods[:, i * model:(i + 1) * model] for i in range(3))
    masks = item_masks(ids)

    x = tokens_in[0].astype(f32)
    mean = jnp.mean(x, axis=1, keepdims=True)
    centered = x - mean
    inv = lax.rsqrt(jnp.mean(centered * centered, axis=1, keepdims=True) + EPS)
    normed = centered * inv
    hidden = (normed * (1.0 + pick(scale)) + pick(shift)).astype(bf16)
    first, hidden, masks = lax.optimization_barrier((first, hidden, masks))
    w_z = gather0(tied(in_weight[:, inner:], first))
    w_o = gather0(tied(out_weight, first))
    first = first.reshape(owners, -1, inner)
    w_x = first if own_model % 16 == 0 else first[:, :own_model].reshape(1, -1, inner)
    pair = jnp.moveaxis(first[:, own_model:].reshape(owners, 2, 2, own_inner, LANES), 0, 2)
    w_xp, w_dt = pair.reshape(2, 2, inner, LANES)
    g = grad_out[0].astype(f32)
    d_branch = (g * pick(gate)).astype(bf16)

    starts = flags.astype(f32)
    starts_b = jnp.concatenate([starts[1:], jnp.ones((1,), f32)])
    calls = [scan_calls(1, length, inner, bool(d)) for d in range(2)]
    project_conv, back_project = projection_calls(length, model, inner, 1 if w_x.shape[0] == 1 else owners)
    wide = lambda v: jnp.broadcast_to(v[None, :, :, None], (1, length, NST, LANES))
    tile = lambda v: jnp.tile(v, (1, SUB))[None]
    xs, *us = project_conv(hidden, w_x, masks, conv_w, conv_b)
    kept = []
    for d in range(2):
        u = us[d]
        proj = mm(u, w_xp[d], ((1,), (0,)))
        dt_low = proj.astype(bf16)
        b_m, c_m = proj[:, rank:rank + NST], proj[:, rank + NST:]
        delta = jax.nn.softplus(mm(dt_low, w_dt[d], ((1,), (1,))) + dt_b[d])
        rate = -jnp.exp(log_rate[d]).T
        rate2 = rate * LOG2E
        sb = jnp.broadcast_to((BIG * (starts_b if d else starts))[None, :, None], (1, length, LANES))
        b_wide = wide(b_m)
        y, ck = calls[d][0](delta[None], u[None], sb, b_wide, tile(c_m), rate2, skip[d][None])
        kept.append((u, dt_low, b_m, c_m, delta, rate, rate2, sb, b_wide, y[0], ck))
    gated, d_scan, d_z = gate_call(length, model, inner)(
        hidden, d_branch, w_z, w_o, kept[0][9], kept[1][9])
    grad_out_w = mm(gated, d_branch, ((0,), (0,))).astype(bf16)
    grad_in_z = mm(hidden, d_z, ((0,), (0,))).astype(bf16)
    d_scan, grad_out_w, grad_in_z = lax.optimization_barrier((d_scan, grad_out_w, grad_in_z))
    over_dp = lambda v: lax.psum_scatter(v, "dp", scatter_dimension=0, tiled=True)
    over_fsdp = lambda v: lax.psum_scatter(v.reshape(-1, model), "fsdp", scatter_dimension=0, tiled=True)
    ranks = lax.axis_size("fsdp")
    halves = lambda v: [h.reshape(ranks, -1, model) for h in jnp.split(v, inner // model, axis=1)]
    joined = lambda v: jnp.concatenate(jnp.split(v, inner // model, axis=0), axis=1)
    early_o, early_z = over_dp(grad_out_w), over_dp(grad_in_z)
    branch = mm(gated, w_o, ((1,), (0,)))
    block_out = (x + pick(gate) * branch).astype(bf16)
    d_gate = g * branch
    lane = lax.broadcasted_iota(jnp.int32, (1, LANES), 1)
    def by_owner(v, dim):
        shape = v.shape[:dim] + (owners, v.shape[dim] // owners) + v.shape[dim + 1:]
        return jnp.moveaxis(v.reshape(shape), dim, 0).astype(bf16)

    def send(values, dims):
        pieces = [by_owner(v, dim) for v, dim in zip(values, dims)]
        flat = jnp.concatenate([p.reshape(owners, -1) for p in pieces], axis=1)
        flat = jnp.pad(flat, ((0, 0), (0, -flat.shape[1] % (8 * LANES)))).reshape(owners, -1, LANES)
        return flat, [p.shape[1:] for p in pieces]

    def exchange(flat):
        return jnp.sum(lax.all_to_all(flat, AXES, 0, 0, tiled=True).astype(f32), axis=0).reshape(-1)

    def receive(own, shapes):
        out, at = [], 0
        for shape in shapes:
            count = 1
            for n in shape:
                count *= n
            out.append(own[at:at + count].reshape(shape))
            at += count
        return out

    d_us, sent = [], []
    carried = d_scan
    for d in range(2):
        u, dt_low, b_m, c_m, delta, rate, rate2, sb, b_wide, _, ck = kept[d]
        du, dr, db, dc, ga, gs, gb = calls[d][1](
            delta[None], u[None], sb, b_wide, wide(c_m), tile(b_m), carried[None], ck, rate, rate2,
            skip[d][None])
        dr = dr[0]
        if d == 1:
            dr, early_o, early_z = lax.optimization_barrier((dr, early_o, early_z))
        d_low = mm(dr, w_dt[d], ((1,), (0,)))
        d_proj = jnp.where(lane < rank, d_low, jnp.where(lane < rank + NST, db[0], dc[0])).astype(bf16)
        g_dt = mm(dr, dt_low, ((0,), (0,)))
        g_xp = mm(u, d_proj, ((0,), (0,)))
        flat, shapes = send((g_xp, g_dt, jnp.sum(gb, axis=0), ga.T, jnp.sum(gs, axis=0)), (0,) * 5)
        d_us.append(du[0] + mm(d_proj, w_xp[d], ((1,), (1,))))
        if d == 0:
            carried, flat = lax.optimization_barrier((carried, flat))
        else:
            d_us[1], flat = lax.optimization_barrier((d_us[1], flat))
        sent.append((flat, shapes))
    packed = jnp.concatenate([s[0].reshape(owners, -1) for s in sent], axis=1)
    span = sent[0][0].size // owners
    packed = jnp.pad(packed, ((0, 0), (0, -packed.shape[1] % (8 * model)))).reshape(-1, model)
    early = over_fsdp(jnp.concatenate([early_o.reshape(ranks, -1, model)] + halves(early_z), axis=1))
    grad_out_w, grad_in_z = early[:own_inner], joined(early[own_inner:])
    packed = over_dp(packed)
    d_xs, g_cw, g_cb = conv_back_call(length, inner)(xs, d_us[0], d_us[1], masks, conv_w, conv_b)
    grad_in_x = mm(hidden, d_xs, ((0,), (0,))).astype(bf16)

    grad_in_x = over_dp(tied(grad_in_x, packed, early))
    flat, shapes = send((g_cw, g_cb), (2, 1))
    g_cw, g_cb = receive(exchange(flat), shapes)

    d_hidden = back_project(d_xs, d_z, w_x, w_z)
    scale_tok = 1.0 + pick(scale)
    d_n = d_hidden * scale_tok
    m1 = jnp.mean(d_n, axis=1, keepdims=True)
    m2 = jnp.mean(d_n * normed, axis=1, keepdims=True)
    grad_tokens = g + (d_n - m1 - normed * m2) * inv
    by_item = lambda v: jnp.stack([jnp.sum(jnp.where(second, 0.0, v), axis=0),
                                   jnp.sum(jnp.where(second, v, 0.0), axis=0)])
    d_mods = jnp.concatenate([by_item(d_hidden), by_item(d_hidden * normed), by_item(d_gate)], axis=1)
    d_mods_all = to_all(d_mods.astype(bf16)).reshape(owners * 2, -1)
    grad_mod_w = mm(act_own, d_mods_all, ((0,), (0,)))
    own_b = mod_bias.shape[0]
    grad_mod_b = jnp.sum(
        lax.dynamic_slice(d_mods_all, (0, me * own_b), (owners * 2, own_b)).astype(f32), axis=0)
    d_act = mm(d_mods_all, mod_weight, ((1,), (1,))).reshape(owners, 2, own_model)
    d_act = lax.all_to_all(d_act, AXES, 0, 0, tiled=True)
    grad_in_x, d_act, g_cw = lax.optimization_barrier((grad_in_x, d_act, g_cw))
    late = over_fsdp(jnp.concatenate(halves(grad_in_x) + [packed.reshape(ranks, -1, model)], axis=1))
    count = own_model * (inner // model)
    grad_in = jnp.concatenate([joined(late[:count]), grad_in_z], axis=1).astype(f32)
    packed = late[count:].reshape(-1)[:2 * span].astype(f32).reshape(2, -1)
    g_xp, g_dt, g_db, g_al, g_sk = [
        jnp.stack(v) for v in zip(*(receive(packed[d], sent[d][1]) for d in range(2)))]
    g_dt = jnp.swapaxes(g_dt[..., :rank], 1, 2)
    d_act = jnp.moveaxis(d_act, 0, 1).reshape(2, model)
    sc = jax.nn.sigmoid(cond)
    grad_cond = d_act * sc * (1.0 + cond * (1.0 - sc))
    return (block_out[None], grad_tokens[None], grad_cond[None], grad_in, grad_out_w.astype(f32), g_xp,
            g_dt, g_cw, g_cb, g_db, g_al, g_sk, grad_mod_w, grad_mod_b)


def solution(mesh):
    row3, row2, row1 = P(AXES, None, None), P(AXES, None), P(AXES)
    mid3, mid2, last3 = P(None, AXES, None), P(None, AXES), P(None, None, AXES)
    weights = (row2, row2, mid3, last3, last3, mid2, mid2, mid3, mid2, row2, row1)
    return jax.shard_map(
        body, mesh=mesh, in_specs=(row3, row3, row2, row3) + weights,
        out_specs=(row3, row3, row3) + weights, check_vma=False)
```

```python
import functools

import jax
import jax.numpy as jnp
from jax import lax
from jax.experimental import pallas as pl
from jax.experimental.pallas import tpu as pltpu
from jax.sharding import PartitionSpec as P

NST = 16
SUB = 16
KCONV = 4
LANES = 128
bf16 = jnp.bfloat16
f32 = jnp.float32


def split_hi_lo(v):
    hi = v.astype(bf16)
    lo = (v - hi.astype(f32)).astype(bf16)
    return jnp.concatenate([hi, lo], axis=0)


def block_diag(tiled):
    rows = lax.broadcasted_iota(jnp.int32, tiled.shape, 0) % SUB
    cols = lax.broadcasted_iota(jnp.int32, tiled.shape, 1) // NST
    return jnp.where(rows == cols, tiled, 0.0)


PAIR = 256


def fold(v):
    v = block_diag(v)
    v = v[:, :LANES] + v[:, LANES:]
    for by in (64, 32, 16):
        v = v + pltpu.roll(v, by, 1)
    return v


def same_state():
    rows = lax.broadcasted_iota(jnp.int32, (NST, SUB * NST), 0)
    cols = lax.broadcasted_iota(jnp.int32, (NST, SUB * NST), 1) % NST
    return jnp.where(rows == cols, 1.0, 0.0).astype(bf16)


def fwd_kernel(delta_ref, u_ref, sb_ref, bx_ref, ct_ref, a2_ref, skip_ref, y_ref, ck_ref,
               h_scr, dx_scr, du_scr, *, backwards, subs, width):
    lane0 = pl.multiple_of(pl.program_id(2) * width, width)

    @pl.when(pl.program_id(1) == 0)
    def _():
        h_scr[:, pl.ds(lane0, width)] = jnp.zeros((NST, width), f32)

    order = range(SUB - 1, -1, -1) if backwards else range(SUB)

    def sub_step(step, carry):
        sub = subs - 1 - step if backwards else step
        row0 = pl.multiple_of(sub * SUB, SUB)
        rows = pl.ds(row0, SUB)
        sb = sb_ref[rows, :]
        sb = jnp.concatenate([sb] * (PAIR // LANES), axis=1)
        c2 = split_hi_lo(block_diag(ct_ref[rows, :]))
        for p in range(width // PAIR):
            lanes = pl.ds(p * PAIR, PAIR)
            glob = pl.ds(lane0 + p * PAIR, PAIR)
            delta = delta_ref[rows, lanes]
            u = u_ref[rows, lanes].astype(f32)
            du_scr[:, lanes] = delta * u
            dx_scr[:, lanes] = delta + sb
            h = h_scr[:, glob]
            a2 = a2_ref[:, glob]
            ck_ref[sub, :, lanes] = h
            states = [None] * SUB
            for t in order:
                b = bx_ref[row0 + t]
                b = jnp.concatenate([b] * (PAIR // LANES), axis=1)
                h = jnp.exp2(dx_scr[pl.ds(t, 1), lanes] * a2) * h + du_scr[pl.ds(t, 1), lanes] * b
                states[t] = h.astype(bf16)
            h_scr[:, glob] = h
            y2 = jnp.dot(c2, jnp.concatenate(states, axis=0), preferred_element_type=f32)
            y_ref[rows, lanes] = y2[:SUB] + y2[SUB:] + skip_ref[:, glob] * u
        return carry

    lax.fori_loop(0, subs, sub_step, 0)


def bwd_kernel(delta_ref, u_ref, sb_ref, bx_ref, cx_ref, bt_ref, ds_ref, ck_ref, a_ref, a2_ref,
               skip_ref, du_out, dr_out, db_out, dc_out, ga_out, gs_out, gb_out,
               g_scr, dx_scr, du_scr, db_scr, dc_scr, *, backwards, subs, width):
    first = pl.program_id(1) == 0
    start = jnp.logical_and(first, pl.program_id(0) == 0)
    eg = pl.program_id(2)
    lane0 = pl.multiple_of(eg * width, width)
    wide = pl.ds(lane0, width)

    @pl.when(first)
    def _():
        g_scr[:, wide] = jnp.zeros((NST, width), f32)

    @pl.when(start)
    def _():
        ga_out[:, wide] = jnp.zeros((NST, width), f32)
        gs_out[:, wide] = jnp.zeros((SUB, width), f32)
        gb_out[:, wide] = jnp.zeros((SUB, width), f32)

    @pl.when(eg == 0)
    def _():
        db_scr[...] = jnp.zeros_like(db_scr)
        dc_scr[...] = jnp.zeros_like(dc_scr)

    order = list(range(SUB - 1, -1, -1) if backwards else range(SUB))
    nt = (((1,), (1,)), ((), ()))
    twice = lambda v: jnp.concatenate([v] * (PAIR // LANES), axis=1)

    def sub_step(step, carry):
        sub = step if backwards else subs - 1 - step
        row0 = pl.multiple_of(sub * SUB, SUB)
        rows = pl.ds(row0, SUB)
        sb = twice(sb_ref[rows, :])
        b2 = split_hi_lo(block_diag(bt_ref[rows, :]))
        ones = block_diag(jnp.ones((SUB, SUB * NST), f32)).astype(bf16)
        pick = same_state()
        db, dc = jnp.zeros((SUB, SUB * NST), f32), jnp.zeros((SUB, SUB * NST), f32)
        for p in range(width // PAIR):
            lanes = pl.ds(p * PAIR, PAIR)
            glob = pl.ds(lane0 + p * PAIR, PAIR)
            delta = delta_ref[rows, lanes]
            u = u_ref[rows, lanes].astype(f32)
            ds = ds_ref[rows, lanes]
            d_in = delta * u
            du_scr[:, lanes] = d_in
            dx_scr[:, lanes] = delta + sb
            a2 = a2_ref[:, glob]
            h = ck_ref[sub, :, lanes]
            decay, states, before = [None] * SUB, [None] * SUB, h.astype(bf16)
            prev = [None] * SUB
            for t in order:
                prev[t] = before
                decay[t] = jnp.exp2(dx_scr[pl.ds(t, 1), lanes] * a2)
                h = decay[t] * h + du_scr[pl.ds(t, 1), lanes] * twice(bx_ref[row0 + t])
                states[t] = before = h.astype(bf16)
            e2 = lax.dot_general(split_hi_lo(ds), jnp.concatenate(states, axis=0), nt,
                                 preferred_element_type=f32)
            dc = dc + (e2[:SUB] + e2[SUB:])
            a = a_ref[:, glob].astype(bf16)
            g = g_scr[:, glob]
            lams, rs, gas = [None] * SUB, [None] * SUB, [None] * SUB
            for t in reversed(order):
                lam = twice(cx_ref[row0 + t]) * ds_ref[pl.ds(row0 + t, 1), lanes] + g
                lams[t] = lam.astype(bf16)
                g = decay[t] * lam
                rs[t] = g.astype(bf16) * prev[t] * a
                gas[t] = rs[t] * jnp.broadcast_to(dx_scr[pl.ds(t, 1), lanes], (NST, PAIR)).astype(bf16)
            g_scr[:, glob] = g
            ga_out[:, glob] += jnp.dot(pick, jnp.concatenate(gas, axis=0), preferred_element_type=f32)
            lams = jnp.concatenate(lams, axis=0)
            s2 = jnp.dot(b2, lams, preferred_element_type=f32)
            s1 = s2[:SUB] + s2[SUB:]
            dd = jnp.dot(ones, jnp.concatenate(rs, axis=0), preferred_element_type=f32) + u * s1
            du_out[rows, lanes] = skip_ref[:, glob] * ds + delta * s1
            small = delta * (1.0 - delta * (0.5 - delta * (1.0 / 6.0)))
            sig = jnp.where(delta < 0.03, small, 1.0 - jnp.exp(-delta))
            dr = dd * sig
            dr_out[rows, lanes] = dr.astype(bf16)
            gb_out[:, glob] += dr
            gs_out[:, glob] += ds * u
            d2 = lax.dot_general(split_hi_lo(d_in), lams, nt, preferred_element_type=f32)
            db = db + (d2[:SUB] + d2[SUB:])
        db_scr[rows, :] += db
        dc_scr[rows, :] += dc
        return carry

    lax.fori_loop(0, subs, sub_step, 0)

    @pl.when(eg == pl.num_programs(2) - 1)
    def _():
        db_out[...] = fold(db_scr[...])
        dc_out[...] = fold(dc_scr[...])


def lane_groups(width_all, widths):
    for width in widths:
        if width_all % width == 0:
            return width
    return width_all


def scan_calls(rows, length, inner, backwards, tblock=128, width=None):
    width = width or lane_groups(inner, (3072, 1536, 1024, 512, 256))
    n_t, n_e, subs = length // tblock, inner // width, tblock // SUB
    params = pltpu.CompilerParams(dimension_semantics=("arbitrary",) * 3)

    def specs(flip):
        tb = (lambda i: n_t - 1 - i) if flip else (lambda i: i)
        tok = pl.BlockSpec((None, tblock, width), lambda r, i, e: (r, tb(i), e))
        lane = pl.BlockSpec((None, tblock, LANES), lambda r, i, e: (r, tb(i), 0))
        exp = pl.BlockSpec((None, tblock, NST, LANES), lambda r, i, e: (r, tb(i), 0, 0))
        til = pl.BlockSpec((None, tblock, SUB * NST), lambda r, i, e: (r, tb(i), 0))
        ck = pl.BlockSpec((None, subs, NST, width), lambda r, i, e: (r, tb(i), 0, e))
        full = pl.BlockSpec((NST, inner), lambda r, i, e: (0, 0))
        one = pl.BlockSpec((1, inner), lambda r, i, e: (0, 0))
        return tok, lane, exp, til, ck, full, one

    sds = jax.ShapeDtypeStruct
    tok, lane, exp, til, ck, full, one = specs(backwards)
    fwd = pl.pallas_call(
        functools.partial(fwd_kernel, backwards=backwards, subs=subs, width=width),
        grid=(rows, n_t, n_e),
        in_specs=[tok, tok, lane, exp, til, full, one],
        out_specs=[tok, ck],
        out_shape=[sds((rows, length, inner), f32), sds((rows, length // SUB, NST, inner), f32)],
        scratch_shapes=[pltpu.VMEM((NST, inner), f32)] + [pltpu.VMEM((SUB, width), f32)] * 2,
        compiler_params=params,
        name="scan_ahead_" + ("b" if backwards else "f"),
    )
    tok, lane, exp, til, ck, full, one = specs(not backwards)
    bwd = pl.pallas_call(
        functools.partial(bwd_kernel, backwards=backwards, subs=subs, width=width),
        grid=(rows, n_t, n_e),
        in_specs=[tok, tok, lane, exp, exp, til, tok, ck, full, full, one],
        out_specs=[tok, tok, lane, lane, full, full, full],
        out_shape=[sds((rows, length, inner), f32), sds((rows, length, inner), bf16),
                   sds((rows, length, LANES), f32), sds((rows, length, LANES), f32),
                   sds((NST, inner), f32), sds((SUB, inner), f32), sds((SUB, inner), f32)],
        scratch_shapes=[pltpu.VMEM((NST, inner), f32)] + [pltpu.VMEM((SUB, width), f32)] * 2
        + [pltpu.VMEM((tblock, SUB * NST), f32)] * 2,
        compiler_params=params,
        name="scan_back_" + ("b" if backwards else "f"),
    )
    return fwd, bwd


def conv_taps(pad_ref, row0, count, sign, masks_ref, lag):
    if lag == 0:
        return pad_ref[pl.ds(row0 + 8, count), :]
    side = 0 if sign > 0 else KCONV - 1
    return pad_ref[pl.ds(row0 + 8 - sign * lag, count), :] * masks_ref[side + lag - 1, pl.ds(row0, count), :]


def fill_padded(pad_ref, length):
    edge = jnp.zeros((8, LANES), f32)
    pad_ref[pl.ds(0, 8), :] = edge
    pad_ref[pl.ds(8 + length, 8), :] = edge


def project_conv_kernel(h_ref, wts_ref, masks_ref, w_ref, b_ref, x_ref, u0_ref, u1_ref, pad_scr,
                        *, length, chunk, width):
    for half in range(width // PAIR):
        cols = pl.ds(half * PAIR, PAIR)
        wts = wts_ref[:, :, cols].reshape(h_ref.shape[1], PAIR)
        x_ref[:, cols] = jnp.dot(h_ref[...], wts, preferred_element_type=f32)
    for tile in range(width // LANES):
        lanes = pl.ds(tile * LANES, LANES)
        pad = pad_scr.at[tile % 2]
        fill_padded(pad, length)
        pad[pl.ds(8, length), :] = x_ref[:, lanes]
        for row0 in range(0, length, chunk):
            for d, (sign, out) in enumerate(((1, u0_ref), (-1, u1_ref))):
                pre = b_ref[d:d + 1, lanes]
                for lag in range(KCONV):
                    tap = conv_taps(pad, row0, chunk, sign, masks_ref, lag)
                    pre = pre + w_ref[d, lag:lag + 1, lanes] * tap
                out[pl.ds(row0, chunk), lanes] = (pre * jax.nn.sigmoid(pre)).astype(bf16)


def back_project_kernel(dx_ref, dz_ref, wx_ref, wz_ref, out_ref, *, width):
    @pl.when(pl.program_id(0) == 0)
    def _():
        out_ref[...] = jnp.zeros_like(out_ref)

    nt = (((1,), (1,)), ((), ()))
    wx = wx_ref[...].reshape(out_ref.shape[1], width)
    out_ref[...] += (lax.dot_general(dx_ref[...], wx, nt, preferred_element_type=f32)
                     + lax.dot_general(dz_ref[...], wz_ref[...], nt, preferred_element_type=f32))


def conv_back_kernel(x_ref, du0_ref, du1_ref, masks_ref, w_ref, b_ref, dx_ref, gw_ref, gb_ref,
                     pad_scr, dp0_scr, dp1_scr, *, length, chunk, tiles):
    both = ((1, du0_ref, dp0_scr), (-1, du1_ref, dp1_scr))
    for tile in range(tiles):
        lanes = pl.ds(tile * LANES, LANES)
        for ref in (pad_scr, dp0_scr, dp1_scr):
            fill_padded(ref, length)
        pad_scr[pl.ds(8, length), :] = x_ref[:, lanes]
        for d, (sign, du_ref, dp_scr) in enumerate(both):
            sums = [jnp.zeros((8, LANES), f32) for _ in range(KCONV + 1)]
            for row0 in range(0, length, chunk):
                taps = [conv_taps(pad_scr, row0, chunk, sign, masks_ref, lag) for lag in range(KCONV)]
                pre = b_ref[d:d + 1, lanes]
                for lag in range(KCONV):
                    pre = pre + w_ref[d, lag:lag + 1, lanes] * taps[lag]
                sg = jax.nn.sigmoid(pre)
                d_pre = du_ref[pl.ds(row0, chunk), lanes] * (sg * (1.0 + pre * (1.0 - sg)))
                dp_scr[pl.ds(row0 + 8, chunk), :] = d_pre
                for lag in range(KCONV + 1):
                    term = d_pre * taps[lag] if lag < KCONV else d_pre
                    sums[lag] = sums[lag] + jnp.sum(term.reshape(chunk // 8, 8, LANES), axis=0)
            for lag in range(KCONV):
                gw_ref[d, lag:lag + 1, lanes] = jnp.sum(sums[lag], axis=0, keepdims=True)
            gb_ref[d:d + 1, lanes] = jnp.sum(sums[KCONV], axis=0, keepdims=True)
        for row0 in range(0, length, chunk):
            total = jnp.zeros((chunk, LANES), f32)
            for d, (sign, _, dp_scr) in enumerate(both):
                for lag in range(KCONV):
                    total = total + w_ref[d, lag:lag + 1, lanes] * conv_taps(
                        dp_scr, row0, chunk, -sign, masks_ref, lag)
            dx_ref[pl.ds(row0, chunk), lanes] = total.astype(bf16)


def gate_kernel(h_ref, g_ref, wz_ref, wo_ref, y0_ref, y1_ref, gated_ref, ds_ref, dz_ref, z_scr, d_scr,
                *, length, chunk):
    z_scr[...] = jnp.dot(h_ref[...], wz_ref[...], preferred_element_type=f32)
    d_scr[...] = lax.dot_general(g_ref[...], wo_ref[...], (((1,), (1,)), ((), ())),
                                 preferred_element_type=f32)
    for row0 in range(0, length, chunk):
        rows = pl.ds(row0, chunk)
        z, d_gated = z_scr[rows, :], d_scr[rows, :]
        both = y0_ref[rows, :] + y1_ref[rows, :]
        sig = jax.nn.sigmoid(z)
        silu = z * sig
        gated_ref[rows, :] = (both * silu).astype(bf16)
        ds_ref[rows, :] = d_gated * silu
        dz_ref[rows, :] = (d_gated * both * sig * (1.0 + z * (1.0 - sig))).astype(bf16)


def gate_call(length, model, inner, width=384, chunk=32):
    if inner % width:
        width = PAIR
    tok = pl.BlockSpec((length, width), lambda e: (0, e))
    every = pl.BlockSpec((length, model), lambda e: (0, 0))
    sds = jax.ShapeDtypeStruct
    return pl.pallas_call(
        functools.partial(gate_kernel, length=length, chunk=chunk), grid=(inner // width,),
        in_specs=[every, every, pl.BlockSpec((model, width), lambda e: (0, e)),
                  pl.BlockSpec((width, model), lambda e: (e, 0)), tok, tok],
        out_specs=[tok, tok, tok],
        out_shape=[sds((length, inner), bf16), sds((length, inner), f32), sds((length, inner), bf16)],
        scratch_shapes=[pltpu.VMEM((length, width), f32)] * 2,
        compiler_params=pltpu.CompilerParams(dimension_semantics=("arbitrary",)), name="gate")


def projection_calls(length, model, inner, blocks, width=512, chunk=64):
    if inner % width:
        width = PAIR
    rows = model // blocks
    tok = pl.BlockSpec((length, width), lambda e: (0, e))
    every = pl.BlockSpec((length, model), lambda e: (0, 0))
    wts = pl.BlockSpec((blocks, rows, width), lambda e: (0, 0, e))
    flat = pl.BlockSpec((model, width), lambda e: (0, e))
    masks = pl.BlockSpec((2 * (KCONV - 1), length, LANES), lambda e: (0, 0, 0))
    taps = pl.BlockSpec((2, KCONV, width), lambda e: (0, 0, e))
    bias = pl.BlockSpec((2, width), lambda e: (0, e))
    sds = jax.ShapeDtypeStruct
    params = pltpu.CompilerParams(dimension_semantics=("arbitrary",))
    ahead = pl.pallas_call(
        functools.partial(project_conv_kernel, length=length, chunk=chunk, width=width),
        grid=(inner // width,), in_specs=[every, wts, masks, taps, bias], out_specs=[tok, tok, tok],
        out_shape=[sds((length, inner), f32)] + [sds((length, inner), bf16)] * 2,
        scratch_shapes=[pltpu.VMEM((2, length + 16, LANES), f32)], compiler_params=params,
        name="project_conv")
    back = pl.pallas_call(
        functools.partial(back_project_kernel, width=width), grid=(inner // width,),
        in_specs=[tok, tok, wts, flat], out_specs=every,
        out_shape=sds((length, model), f32), compiler_params=params, name="back_project")
    return ahead, back


def conv_back_call(length, inner, width=256, chunk=64):
    if inner % width:
        width = LANES
    tok = pl.BlockSpec((length, width), lambda e: (0, e))
    masks = pl.BlockSpec((2 * (KCONV - 1), length, LANES), lambda e: (0, 0, 0))
    taps = pl.BlockSpec((2, KCONV, width), lambda e: (0, 0, e))
    bias = pl.BlockSpec((2, width), lambda e: (0, e))
    sds = jax.ShapeDtypeStruct
    pad = pltpu.VMEM((length + 16, LANES), f32)
    sizes = dict(length=length, chunk=chunk, tiles=width // LANES)
    params = pltpu.CompilerParams(dimension_semantics=("arbitrary",))
    back = pl.pallas_call(
        functools.partial(conv_back_kernel, **sizes), grid=(inner // width,),
        in_specs=[tok, tok, tok, masks, taps, bias], out_specs=[tok, taps, bias],
        out_shape=[sds((length, inner), bf16), sds((2, KCONV, inner), f32), sds((2, inner), f32)],
        scratch_shapes=[pad] * 3, compiler_params=params, name="conv_back")
    return back


EPS = 1e-06
AXES = ("dp", "fsdp")
BIG = 1e30
LOG2E = 1.4426950408889634


def mm(a, b, dims):
    return lax.dot_general(a, b, (dims, ((), ())), preferred_element_type=f32)


def to_all(v):
    owners = lax.axis_size(AXES)
    return lax.all_to_all(jnp.broadcast_to(v[None], (owners,) + v.shape), AXES, 0, 0, tiled=True)


def gather0(v):
    return lax.all_gather(v, AXES, axis=0, tiled=True)


def tied(v, *after):
    return lax.optimization_barrier((v,) + after)[0]


def item_masks(ids):
    length = ids.shape[0]
    pad = jnp.full((KCONV - 1,), -1, ids.dtype)
    long = jnp.concatenate([pad, ids, pad])
    shifts = [-lag for lag in range(1, KCONV)] + list(range(1, KCONV))
    rows = [(long[KCONV - 1 + s:KCONV - 1 + s + length] == ids).astype(f32) for s in shifts]
    return jnp.broadcast_to(jnp.stack(rows)[:, :, None], (len(rows), length, LANES))


def body(tokens_in, condition, item_flags, grad_out, in_weight, out_weight, x_projection,
         dt_projection, conv_weight, conv_bias, dt_bias, decay_log, skip_gain, mod_weight, mod_bias):
    length, model = tokens_in.shape[1:]
    owners = lax.axis_size(AXES)
    me = lax.axis_index(AXES)
    inner = in_weight.shape[1] // 2
    own_model = in_weight.shape[0]
    rank = dt_projection.shape[1]

    own_inner = out_weight.shape[0]
    side = jnp.pad(jnp.swapaxes(dt_projection, 1, 2), ((0, 0), (0, 0), (0, LANES - rank)))
    pair = jnp.stack([x_projection, side])
    first = gather0(jnp.concatenate([in_weight[:, :inner], pair.reshape(-1, inner)], axis=0))

    cond = condition[0].astype(f32)
    act = jax.nn.silu(cond).astype(bf16)
    smalls = (act, conv_weight, conv_bias, dt_bias, decay_log, skip_gain, mod_bias)
    flat = jnp.concatenate([v.reshape(-1) for v in smalls])
    flat = jnp.pad(flat, (0, -flat.shape[0] % (8 * LANES)))
    everyone = to_all(flat.reshape(-1, LANES)).reshape(owners, -1)
    parts, at = [], 0
    for v in smalls:
        parts.append(everyone[:, at:at + v.size].reshape((owners,) + v.shape))
        at += v.size
    act_all = parts[0].reshape(owners * 2, model)
    join = lambda v, dim: jnp.moveaxis(v, 0, dim).reshape(
        v.shape[1:dim + 1] + (owners * v.shape[dim + 1],) + v.shape[dim + 2:]).astype(f32)
    conv_w, conv_b, dt_b = join(parts[1], 2), join(parts[2], 1), join(parts[3], 1)
    log_rate, skip = join(parts[4], 1), join(parts[5], 1)
    modb = parts[6].reshape(-1).astype(f32)

    act_own = lax.dynamic_slice(act_all, (0, me * own_model), (owners * 2, own_model))
    partial = mm(act_own, mod_weight, ((1,), (0,))).reshape(owners, 2, -1)
    mods = jnp.sum(lax.all_to_all(partial, AXES, 0, 0, tiled=True), axis=0) + modb
    flags = item_flags[0]
    ids = jnp.cumsum(flags, dtype=jnp.int32) - 1
    second = (ids == 1)[:, None]
    pick = lambda v: jnp.where(second, v[1], v[0])
    shift, scale, gate = (mods[:, i * model:(i + 1) * model] for i in range(3))
    masks = item_masks(ids)

    x = tokens_in[0].astype(f32)
    mean = jnp.mean(x, axis=1, keepdims=True)
    centered = x - mean
    inv = lax.rsqrt(jnp.mean(centered * centered, axis=1, keepdims=True) + EPS)
    normed = centered * inv
    hidden = (normed * (1.0 + pick(scale)) + pick(shift)).astype(bf16)
    first, hidden, masks = lax.optimization_barrier((first, hidden, masks))
    w_z = gather0(tied(in_weight[:, inner:], first))
    w_o = gather0(tied(out_weight, first))
    first = first.reshape(owners, -1, inner)
    w_x = first if own_model % 16 == 0 else first[:, :own_model].reshape(1, -1, inner)
    pair = jnp.moveaxis(first[:, own_model:].reshape(owners, 2, 2, own_inner, LANES), 0, 2)
    w_xp, w_dt = pair.reshape(2, 2, inner, LANES)
    g = grad_out[0].astype(f32)
    d_branch = (g * pick(gate)).astype(bf16)

    starts = flags.astype(f32)
    starts_b = jnp.concatenate([starts[1:], jnp.ones((1,), f32)])
    calls = [scan_calls(1, length, inner, bool(d)) for d in range(2)]
    project_conv, back_project = projection_calls(length, model, inner, 1 if w_x.shape[0] == 1 else owners)
    wide = lambda v: jnp.broadcast_to(v[None, :, :, None], (1, length, NST, LANES))
    tile = lambda v: jnp.tile(v, (1, SUB))[None]
    xs, *us = project_conv(hidden, w_x, masks, conv_w, conv_b)
    kept = []
    for d in range(2):
        u = us[d]
        proj = mm(u, w_xp[d], ((1,), (0,)))
        dt_low = proj.astype(bf16)
        b_m, c_m = proj[:, rank:rank + NST], proj[:, rank + NST:]
        delta = jax.nn.softplus(mm(dt_low, w_dt[d], ((1,), (1,))) + dt_b[d])
        rate = -jnp.exp(log_rate[d]).T
        rate2 = rate * LOG2E
        sb = jnp.broadcast_to((BIG * (starts_b if d else starts))[None, :, None], (1, length, LANES))
        b_wide = wide(b_m)
        y, ck = calls[d][0](delta[None], u[None], sb, b_wide, tile(c_m), rate2, skip[d][None])
        kept.append((u, dt_low, b_m, c_m, delta, rate, rate2, sb, b_wide, y[0], ck))
    gated, d_scan, d_z = gate_call(length, model, inner)(
        hidden, d_branch, w_z, w_o, kept[0][9], kept[1][9])
    grad_out_w = mm(gated, d_branch, ((0,), (0,))).astype(bf16)
    grad_in_z = mm(hidden, d_z, ((0,), (0,))).astype(bf16)
    d_scan, grad_out_w, grad_in_z = lax.optimization_barrier((d_scan, grad_out_w, grad_in_z))
    over_dp = lambda v: lax.psum_scatter(v, "dp", scatter_dimension=0, tiled=True)
    over_fsdp = lambda v: lax.psum_scatter(v.reshape(-1, model), "fsdp", scatter_dimension=0, tiled=True)
    ranks = lax.axis_size("fsdp")
    halves = lambda v: [h.reshape(ranks, -1, model) for h in jnp.split(v, inner // model, axis=1)]
    joined = lambda v: jnp.concatenate(jnp.split(v, inner // model, axis=0), axis=1)
    early_o, early_z = over_dp(grad_out_w), over_dp(grad_in_z)
    branch = mm(gated, w_o, ((1,), (0,)))
    block_out = (x + pick(gate) * branch).astype(bf16)
    d_gate = g * branch
    lane = lax.broadcasted_iota(jnp.int32, (1, LANES), 1)
    def by_owner(v, dim):
        shape = v.shape[:dim] + (owners, v.shape[dim] // owners) + v.shape[dim + 1:]
        return jnp.moveaxis(v.reshape(shape), dim, 0).astype(bf16)

    def send(values, dims):
        pieces = [by_owner(v, dim) for v, dim in zip(values, dims)]
        flat = jnp.concatenate([p.reshape(owners, -1) for p in pieces], axis=1)
        flat = jnp.pad(flat, ((0, 0), (0, -flat.shape[1] % (8 * LANES)))).reshape(owners, -1, LANES)
        return flat, [p.shape[1:] for p in pieces]

    def exchange(flat):
        return jnp.sum(lax.all_to_all(flat, AXES, 0, 0, tiled=True).astype(f32), axis=0).reshape(-1)

    def receive(own, shapes):
        out, at = [], 0
        for shape in shapes:
            count = 1
            for n in shape:
                count *= n
            out.append(own[at:at + count].reshape(shape))
            at += count
        return out

    d_us, sent = [], []
    carried = d_scan
    for d in range(2):
        u, dt_low, b_m, c_m, delta, rate, rate2, sb, b_wide, _, ck = kept[d]
        du, dr, db, dc, ga, gs, gb = calls[d][1](
            delta[None], u[None], sb, b_wide, wide(c_m), tile(b_m), carried[None], ck, rate, rate2,
            skip[d][None])
        dr = dr[0]
        if d == 1:
            early = jnp.concatenate([early_o.reshape(ranks, -1, model)] + halves(early_z), axis=1)
            dr, early = lax.optimization_barrier((dr, early))
        d_low = mm(dr, w_dt[d], ((1,), (0,)))
        d_proj = jnp.where(lane < rank, d_low, jnp.where(lane < rank + NST, db[0], dc[0])).astype(bf16)
        g_dt = mm(dr, dt_low, ((0,), (0,)))
        g_xp = mm(u, d_proj, ((0,), (0,)))
        flat, shapes = send((g_xp, g_dt, jnp.sum(gb, axis=0), ga.T, jnp.sum(gs, axis=0)), (0,) * 5)
        d_us.append(du[0] + mm(d_proj, w_xp[d], ((1,), (1,))))
        if d == 0:
            carried, flat = lax.optimization_barrier((carried, flat))
        else:
            d_us[1], flat = lax.optimization_barrier((d_us[1], flat))
        sent.append((flat, shapes))
    packed = jnp.concatenate([s[0].reshape(owners, -1) for s in sent], axis=1)
    span = sent[0][0].size // owners
    packed = jnp.pad(packed, ((0, 0), (0, -packed.shape[1] % (8 * model)))).reshape(-1, model)
    early = over_fsdp(early)
    grad_out_w, grad_in_z = early[:own_inner], joined(early[own_inner:])
    packed = over_dp(packed)
    d_xs, g_cw, g_cb = conv_back_call(length, inner)(xs, d_us[0], d_us[1], masks, conv_w, conv_b)
    grad_in_x = mm(hidden, d_xs, ((0,), (0,))).astype(bf16)

    grad_in_x = over_dp(tied(grad_in_x, packed, early))
    flat, shapes = send((g_cw, g_cb), (2, 1))
    g_cw, g_cb = receive(exchange(flat), shapes)

    d_hidden = back_project(d_xs, d_z, w_x, w_z)
    scale_tok = 1.0 + pick(scale)
    d_n = d_hidden * scale_tok
    m1 = jnp.mean(d_n, axis=1, keepdims=True)
    m2 = jnp.mean(d_n * normed, axis=1, keepdims=True)
    grad_tokens = g + (d_n - m1 - normed * m2) * inv
    by_item = lambda v: jnp.stack([jnp.sum(jnp.where(second, 0.0, v), axis=0),
                                   jnp.sum(jnp.where(second, v, 0.0), axis=0)])
    d_mods = jnp.concatenate([by_item(d_hidden), by_item(d_hidden * normed), by_item(d_gate)], axis=1)
    d_mods_all = to_all(d_mods.astype(bf16)).reshape(owners * 2, -1)
    grad_mod_w = mm(act_own, d_mods_all, ((0,), (0,)))
    own_b = mod_bias.shape[0]
    grad_mod_b = jnp.sum(
        lax.dynamic_slice(d_mods_all, (0, me * own_b), (owners * 2, own_b)).astype(f32), axis=0)
    d_act = mm(d_mods_all, mod_weight, ((1,), (1,))).reshape(owners, 2, own_model)
    d_act = lax.all_to_all(d_act, AXES, 0, 0, tiled=True)
    grad_in_x, d_act, g_cw = lax.optimization_barrier((grad_in_x, d_act, g_cw))
    late = over_fsdp(jnp.concatenate(halves(grad_in_x) + [packed.reshape(ranks, -1, model)], axis=1))
    count = own_model * (inner // model)
    grad_in = jnp.concatenate([joined(late[:count]), grad_in_z], axis=1).astype(f32)
    packed = late[count:].reshape(-1)[:2 * span].astype(f32).reshape(2, -1)
    g_xp, g_dt, g_db, g_al, g_sk = [
        jnp.stack(v) for v in zip(*(receive(packed[d], sent[d][1]) for d in range(2)))]
    g_dt = jnp.swapaxes(g_dt[..., :rank], 1, 2)
    d_act = jnp.moveaxis(d_act, 0, 1).reshape(2, model)
    sc = jax.nn.sigmoid(cond)
    grad_cond = d_act * sc * (1.0 + cond * (1.0 - sc))
    return (block_out[None], grad_tokens[None], grad_cond[None], grad_in, grad_out_w.astype(f32), g_xp,
            g_dt, g_cw, g_cb, g_db, g_al, g_sk, grad_mod_w, grad_mod_b)


def solution(mesh):
    row3, row2, row1 = P(AXES, None, None), P(AXES, None), P(AXES)
    mid3, mid2, last3 = P(None, AXES, None), P(None, AXES), P(None, None, AXES)
    weights = (row2, row2, mid3, last3, last3, mid2, mid2, mid3, mid2, row2, row1)
    return jax.shard_map(
        body, mesh=mesh, in_specs=(row3, row3, row2, row3) + weights,
        out_specs=(row3, row3, row3) + weights, check_vma=False)
```

```python
import functools

import jax
import jax.numpy as jnp
from jax import lax
from jax.experimental import pallas as pl
from jax.experimental.pallas import tpu as pltpu
from jax.sharding import PartitionSpec as P

NST = 16
SUB = 16
KCONV = 4
LANES = 128
bf16 = jnp.bfloat16
f32 = jnp.float32


def split_hi_lo(v):
    hi = v.astype(bf16)
    lo = (v - hi.astype(f32)).astype(bf16)
    return jnp.concatenate([hi, lo], axis=0)


def block_diag(tiled):
    rows = lax.broadcasted_iota(jnp.int32, tiled.shape, 0) % SUB
    cols = lax.broadcasted_iota(jnp.int32, tiled.shape, 1) // NST
    return jnp.where(rows == cols, tiled, 0.0)


PAIR = 256


def fold(v):
    v = block_diag(v)
    v = v[:, :LANES] + v[:, LANES:]
    for by in (64, 32, 16):
        v = v + pltpu.roll(v, by, 1)
    return v


def same_state():
    rows = lax.broadcasted_iota(jnp.int32, (NST, SUB * NST), 0)
    cols = lax.broadcasted_iota(jnp.int32, (NST, SUB * NST), 1) % NST
    return jnp.where(rows == cols, 1.0, 0.0).astype(bf16)


def fwd_kernel(delta_ref, u_ref, sb_ref, bx_ref, ct_ref, a2_ref, skip_ref, y_ref, ck_ref,
               h_scr, dx_scr, du_scr, *, backwards, subs, width):
    lane0 = pl.multiple_of(pl.program_id(2) * width, width)

    @pl.when(pl.program_id(1) == 0)
    def _():
        h_scr[:, pl.ds(lane0, width)] = jnp.zeros((NST, width), f32)

    order = range(SUB - 1, -1, -1) if backwards else range(SUB)

    def sub_step(step, carry):
        sub = subs - 1 - step if backwards else step
        row0 = pl.multiple_of(sub * SUB, SUB)
        rows = pl.ds(row0, SUB)
        sb = sb_ref[rows, :]
        sb = jnp.concatenate([sb] * (PAIR // LANES), axis=1)
        c2 = split_hi_lo(block_diag(ct_ref[rows, :]))
        for p in range(width // PAIR):
            lanes = pl.ds(p * PAIR, PAIR)
            glob = pl.ds(lane0 + p * PAIR, PAIR)
            delta = delta_ref[rows, lanes]
            u = u_ref[rows, lanes].astype(f32)
            du_scr[:, lanes] = delta * u
            dx_scr[:, lanes] = delta + sb
            h = h_scr[:, glob]
            a2 = a2_ref[:, glob]
            ck_ref[sub, :, lanes] = h
            states = [None] * SUB
            for t in order:
                b = bx_ref[row0 + t]
                b = jnp.concatenate([b] * (PAIR // LANES), axis=1)
                h = jnp.exp2(dx_scr[pl.ds(t, 1), lanes] * a2) * h + du_scr[pl.ds(t, 1), lanes] * b
                states[t] = h.astype(bf16)
            h_scr[:, glob] = h
            y2 = jnp.dot(c2, jnp.concatenate(states, axis=0), preferred_element_type=f32)
            y_ref[rows, lanes] = y2[:SUB] + y2[SUB:] + skip_ref[:, glob] * u
        return carry

    lax.fori_loop(0, subs, sub_step, 0)


def bwd_kernel(delta_ref, u_ref, sb_ref, bx_ref, cx_ref, bt_ref, ds_ref, ck_ref, a_ref, a2_ref,
               skip_ref, du_out, dr_out, db_out, dc_out, ga_out, gs_out, gb_out,
               g_scr, dx_scr, du_scr, db_scr, dc_scr, *, backwards, subs, width):
    first = pl.program_id(1) == 0
    start = jnp.logical_and(first, pl.program_id(0) == 0)
    eg = pl.program_id(2)
    lane0 = pl.multiple_of(eg * width, width)
    wide = pl.ds(lane0, width)

    @pl.when(first)
    def _():
        g_scr[:, wide] = jnp.zeros((NST, width), f32)

    @pl.when(start)
    def _():
        ga_out[:, wide] = jnp.zeros((NST, width), f32)
        gs_out[:, wide] = jnp.zeros((SUB, width), f32)
        gb_out[:, wide] = jnp.zeros((SUB, width), f32)

    @pl.when(eg == 0)
    def _():
        db_scr[...] = jnp.zeros_like(db_scr)
        dc_scr[...] = jnp.zeros_like(dc_scr)

    order = list(range(SUB - 1, -1, -1) if backwards else range(SUB))
    nt = (((1,), (1,)), ((), ()))
    twice = lambda v: jnp.concatenate([v] * (PAIR // LANES), axis=1)

    def sub_step(step, carry):
        sub = step if backwards else subs - 1 - step
        row0 = pl.multiple_of(sub * SUB, SUB)
        rows = pl.ds(row0, SUB)
        sb = twice(sb_ref[rows, :])
        b2 = split_hi_lo(block_diag(bt_ref[rows, :]))
        ones = block_diag(jnp.ones((SUB, SUB * NST), f32)).astype(bf16)
        pick = same_state()
        db, dc = jnp.zeros((SUB, SUB * NST), f32), jnp.zeros((SUB, SUB * NST), f32)
        for p in range(width // PAIR):
            lanes = pl.ds(p * PAIR, PAIR)
            glob = pl.ds(lane0 + p * PAIR, PAIR)
            delta = delta_ref[rows, lanes]
            u = u_ref[rows, lanes].astype(f32)
            ds = ds_ref[rows, lanes]
            d_in = delta * u
            du_scr[:, lanes] = d_in
            dx_scr[:, lanes] = delta + sb
            a2 = a2_ref[:, glob]
            h = ck_ref[sub, :, lanes]
            decay, states, before = [None] * SUB, [None] * SUB, h.astype(bf16)
            prev = [None] * SUB
            for t in order:
                prev[t] = before
                decay[t] = jnp.exp2(dx_scr[pl.ds(t, 1), lanes] * a2)
                h = decay[t] * h + du_scr[pl.ds(t, 1), lanes] * twice(bx_ref[row0 + t])
                states[t] = before = h.astype(bf16)
            e2 = lax.dot_general(split_hi_lo(ds), jnp.concatenate(states, axis=0), nt,
                                 preferred_element_type=f32)
            dc = dc + (e2[:SUB] + e2[SUB:])
            a = a_ref[:, glob].astype(bf16)
            g = g_scr[:, glob]
            lams, rs, gas = [None] * SUB, [None] * SUB, [None] * SUB
            for t in reversed(order):
                lam = twice(cx_ref[row0 + t]) * ds_ref[pl.ds(row0 + t, 1), lanes] + g
                lams[t] = lam.astype(bf16)
                g = decay[t] * lam
                rs[t] = g.astype(bf16) * prev[t] * a
                gas[t] = rs[t] * jnp.broadcast_to(dx_scr[pl.ds(t, 1), lanes], (NST, PAIR)).astype(bf16)
            g_scr[:, glob] = g
            ga_out[:, glob] += jnp.dot(pick, jnp.concatenate(gas, axis=0), preferred_element_type=f32)
            lams = jnp.concatenate(lams, axis=0)
            s2 = jnp.dot(b2, lams, preferred_element_type=f32)
            s1 = s2[:SUB] + s2[SUB:]
            dd = jnp.dot(ones, jnp.concatenate(rs, axis=0), preferred_element_type=f32) + u * s1
            du_out[rows, lanes] = skip_ref[:, glob] * ds + delta * s1
            small = delta * (1.0 - delta * (0.5 - delta * (1.0 / 6.0)))
            sig = jnp.where(delta < 0.03, small, 1.0 - jnp.exp(-delta))
            dr = dd * sig
            dr_out[rows, lanes] = dr.astype(bf16)
            gb_out[:, glob] += dr
            gs_out[:, glob] += ds * u
            d2 = lax.dot_general(split_hi_lo(d_in), lams, nt, preferred_element_type=f32)
            db = db + (d2[:SUB] + d2[SUB:])
        db_scr[rows, :] += db
        dc_scr[rows, :] += dc
        return carry

    lax.fori_loop(0, subs, sub_step, 0)

    @pl.when(eg == pl.num_programs(2) - 1)
    def _():
        db_out[...] = fold(db_scr[...])
        dc_out[...] = fold(dc_scr[...])


def lane_groups(width_all, widths):
    for width in widths:
        if width_all % width == 0:
            return width
    return width_all


def scan_calls(rows, length, inner, backwards, tblock=128, width=None):
    width = width or lane_groups(inner, (3072, 1536, 1024, 512, 256))
    n_t, n_e, subs = length // tblock, inner // width, tblock // SUB
    params = pltpu.CompilerParams(dimension_semantics=("arbitrary",) * 3)

    def specs(flip):
        tb = (lambda i: n_t - 1 - i) if flip else (lambda i: i)
        tok = pl.BlockSpec((None, tblock, width), lambda r, i, e: (r, tb(i), e))
        lane = pl.BlockSpec((None, tblock, LANES), lambda r, i, e: (r, tb(i), 0))
        exp = pl.BlockSpec((None, tblock, NST, LANES), lambda r, i, e: (r, tb(i), 0, 0))
        til = pl.BlockSpec((None, tblock, SUB * NST), lambda r, i, e: (r, tb(i), 0))
        ck = pl.BlockSpec((None, subs, NST, width), lambda r, i, e: (r, tb(i), 0, e))
        full = pl.BlockSpec((NST, inner), lambda r, i, e: (0, 0))
        one = pl.BlockSpec((1, inner), lambda r, i, e: (0, 0))
        return tok, lane, exp, til, ck, full, one

    sds = jax.ShapeDtypeStruct
    tok, lane, exp, til, ck, full, one = specs(backwards)
    fwd = pl.pallas_call(
        functools.partial(fwd_kernel, backwards=backwards, subs=subs, width=width),
        grid=(rows, n_t, n_e),
        in_specs=[tok, tok, lane, exp, til, full, one],
        out_specs=[tok, ck],
        out_shape=[sds((rows, length, inner), f32), sds((rows, length // SUB, NST, inner), f32)],
        scratch_shapes=[pltpu.VMEM((NST, inner), f32)] + [pltpu.VMEM((SUB, width), f32)] * 2,
        compiler_params=params,
        name="scan_ahead_" + ("b" if backwards else "f"),
    )
    tok, lane, exp, til, ck, full, one = specs(not backwards)
    bwd = pl.pallas_call(
        functools.partial(bwd_kernel, backwards=backwards, subs=subs, width=width),
        grid=(rows, n_t, n_e),
        in_specs=[tok, tok, lane, exp, exp, til, tok, ck, full, full, one],
        out_specs=[tok, tok, lane, lane, full, full, full],
        out_shape=[sds((rows, length, inner), f32), sds((rows, length, inner), bf16),
                   sds((rows, length, LANES), f32), sds((rows, length, LANES), f32),
                   sds((NST, inner), f32), sds((SUB, inner), f32), sds((SUB, inner), f32)],
        scratch_shapes=[pltpu.VMEM((NST, inner), f32)] + [pltpu.VMEM((SUB, width), f32)] * 2
        + [pltpu.VMEM((tblock, SUB * NST), f32)] * 2,
        compiler_params=params,
        name="scan_back_" + ("b" if backwards else "f"),
    )
    return fwd, bwd


def conv_taps(pad_ref, row0, count, sign, masks_ref, lag):
    if lag == 0:
        return pad_ref[pl.ds(row0 + 8, count), :]
    side = 0 if sign > 0 else KCONV - 1
    return pad_ref[pl.ds(row0 + 8 - sign * lag, count), :] * masks_ref[side + lag - 1, pl.ds(row0, count), :]


def fill_padded(pad_ref, length):
    edge = jnp.zeros((8, LANES), f32)
    pad_ref[pl.ds(0, 8), :] = edge
    pad_ref[pl.ds(8 + length, 8), :] = edge


def project_conv_kernel(h_ref, wts_ref, masks_ref, w_ref, b_ref, x_ref, u0_ref, u1_ref, pad_scr,
                        *, length, chunk, width):
    for half in range(width // PAIR):
        cols = pl.ds(half * PAIR, PAIR)
        wts = wts_ref[:, :, cols].reshape(h_ref.shape[1], PAIR)
        x_ref[:, cols] = jnp.dot(h_ref[...], wts, preferred_element_type=f32)
    for tile in range(width // LANES):
        lanes = pl.ds(tile * LANES, LANES)
        pad = pad_scr.at[tile % 2]
        fill_padded(pad, length)
        pad[pl.ds(8, length), :] = x_ref[:, lanes]
        for row0 in range(0, length, chunk):
            for d, (sign, out) in enumerate(((1, u0_ref), (-1, u1_ref))):
                pre = b_ref[d:d + 1, lanes]
                for lag in range(KCONV):
                    tap = conv_taps(pad, row0, chunk, sign, masks_ref, lag)
                    pre = pre + w_ref[d, lag:lag + 1, lanes] * tap
                out[pl.ds(row0, chunk), lanes] = (pre * jax.nn.sigmoid(pre)).astype(bf16)


def back_project_kernel(dx_ref, dz_ref, wx_ref, wz_ref, out_ref, *, width):
    @pl.when(pl.program_id(0) == 0)
    def _():
        out_ref[...] = jnp.zeros_like(out_ref)

    nt = (((1,), (1,)), ((), ()))
    wx = wx_ref[...].reshape(out_ref.shape[1], width)
    out_ref[...] += (lax.dot_general(dx_ref[...], wx, nt, preferred_element_type=f32)
                     + lax.dot_general(dz_ref[...], wz_ref[...], nt, preferred_element_type=f32))


def conv_back_kernel(x_ref, du0_ref, du1_ref, masks_ref, w_ref, b_ref, dx_ref, gw_ref, gb_ref,
                     pad_scr, dp0_scr, dp1_scr, *, length, chunk, tiles):
    both = ((1, du0_ref, dp0_scr), (-1, du1_ref, dp1_scr))
    for tile in range(tiles):
        lanes = pl.ds(tile * LANES, LANES)
        for ref in (pad_scr, dp0_scr, dp1_scr):
            fill_padded(ref, length)
        pad_scr[pl.ds(8, length), :] = x_ref[:, lanes]
        for d, (sign, du_ref, dp_scr) in enumerate(both):
            sums = [jnp.zeros((8, LANES), f32) for _ in range(KCONV + 1)]
            for row0 in range(0, length, chunk):
                taps = [conv_taps(pad_scr, row0, chunk, sign, masks_ref, lag) for lag in range(KCONV)]
                pre = b_ref[d:d + 1, lanes]
                for lag in range(KCONV):
                    pre = pre + w_ref[d, lag:lag + 1, lanes] * taps[lag]
                sg = jax.nn.sigmoid(pre)
                d_pre = du_ref[pl.ds(row0, chunk), lanes] * (sg * (1.0 + pre * (1.0 - sg)))
                dp_scr[pl.ds(row0 + 8, chunk), :] = d_pre
                for lag in range(KCONV + 1):
                    term = d_pre * taps[lag] if lag < KCONV else d_pre
                    sums[lag] = sums[lag] + jnp.sum(term.reshape(chunk // 8, 8, LANES), axis=0)
            for lag in range(KCONV):
                gw_ref[d, lag:lag + 1, lanes] = jnp.sum(sums[lag], axis=0, keepdims=True)
            gb_ref[d:d + 1, lanes] = jnp.sum(sums[KCONV], axis=0, keepdims=True)
        for row0 in range(0, length, chunk):
            total = jnp.zeros((chunk, LANES), f32)
            for d, (sign, _, dp_scr) in enumerate(both):
                for lag in range(KCONV):
                    total = total + w_ref[d, lag:lag + 1, lanes] * conv_taps(
                        dp_scr, row0, chunk, -sign, masks_ref, lag)
            dx_ref[pl.ds(row0, chunk), lanes] = total.astype(bf16)


def gate_kernel(h_ref, wz_ref, y0_ref, y1_ref, gated_ref, silu_ref, slope_ref, *, length, chunk):
    silu_ref[...] = jnp.dot(h_ref[...], wz_ref[...], preferred_element_type=f32)
    for row0 in range(0, length, chunk):
        rows = pl.ds(row0, chunk)
        z = silu_ref[rows, :]
        both = y0_ref[rows, :] + y1_ref[rows, :]
        sig = jax.nn.sigmoid(z)
        silu = z * sig
        gated_ref[rows, :] = (both * silu).astype(bf16)
        silu_ref[rows, :] = silu
        slope_ref[rows, :] = both * sig * (1.0 + z * (1.0 - sig))


def gate_back_kernel(g_ref, wo_ref, silu_ref, slope_ref, ds_ref, dz_ref, *, length, chunk):
    ds_ref[...] = lax.dot_general(g_ref[...], wo_ref[...], (((1,), (1,)), ((), ())),
                                  preferred_element_type=f32)
    for row0 in range(0, length, chunk):
        rows = pl.ds(row0, chunk)
        d_gated = ds_ref[rows, :]
        ds_ref[rows, :] = d_gated * silu_ref[rows, :]
        dz_ref[rows, :] = (d_gated * slope_ref[rows, :]).astype(bf16)


def gate_calls(length, model, inner, width=384, chunk=32):
    if inner % width:
        width = PAIR
    tok = pl.BlockSpec((length, width), lambda e: (0, e))
    every = pl.BlockSpec((length, model), lambda e: (0, 0))
    low = jax.ShapeDtypeStruct((length, inner), bf16)
    high = jax.ShapeDtypeStruct((length, inner), f32)
    params = pltpu.CompilerParams(dimension_semantics=("arbitrary",))
    ahead = pl.pallas_call(
        functools.partial(gate_kernel, length=length, chunk=chunk), grid=(inner // width,),
        in_specs=[every, pl.BlockSpec((model, width), lambda e: (0, e)), tok, tok],
        out_specs=[tok, tok, tok], out_shape=[low, high, high], compiler_params=params, name="gate")
    back = pl.pallas_call(
        functools.partial(gate_back_kernel, length=length, chunk=chunk), grid=(inner // width,),
        in_specs=[every, pl.BlockSpec((width, model), lambda e: (e, 0)), tok, tok],
        out_specs=[tok, tok], out_shape=[high, low], compiler_params=params, name="gate_back")
    return ahead, back


def projection_calls(length, model, inner, blocks, width=512, chunk=64):
    if inner % width:
        width = PAIR
    rows = model // blocks
    tok = pl.BlockSpec((length, width), lambda e: (0, e))
    every = pl.BlockSpec((length, model), lambda e: (0, 0))
    wts = pl.BlockSpec((blocks, rows, width), lambda e: (0, 0, e))
    flat = pl.BlockSpec((model, width), lambda e: (0, e))
    masks = pl.BlockSpec((2 * (KCONV - 1), length, LANES), lambda e: (0, 0, 0))
    taps = pl.BlockSpec((2, KCONV, width), lambda e: (0, 0, e))
    bias = pl.BlockSpec((2, width), lambda e: (0, e))
    sds = jax.ShapeDtypeStruct
    params = pltpu.CompilerParams(dimension_semantics=("arbitrary",))
    ahead = pl.pallas_call(
        functools.partial(project_conv_kernel, length=length, chunk=chunk, width=width),
        grid=(inner // width,), in_specs=[every, wts, masks, taps, bias], out_specs=[tok, tok, tok],
        out_shape=[sds((length, inner), f32)] + [sds((length, inner), bf16)] * 2,
        scratch_shapes=[pltpu.VMEM((2, length + 16, LANES), f32)], compiler_params=params,
        name="project_conv")
    back = pl.pallas_call(
        functools.partial(back_project_kernel, width=width), grid=(inner // width,),
        in_specs=[tok, tok, wts, flat], out_specs=every,
        out_shape=sds((length, model), f32), compiler_params=params, name="back_project")
    return ahead, back


def conv_back_call(length, inner, width=256, chunk=64):
    if inner % width:
        width = LANES
    tok = pl.BlockSpec((length, width), lambda e: (0, e))
    masks = pl.BlockSpec((2 * (KCONV - 1), length, LANES), lambda e: (0, 0, 0))
    taps = pl.BlockSpec((2, KCONV, width), lambda e: (0, 0, e))
    bias = pl.BlockSpec((2, width), lambda e: (0, e))
    sds = jax.ShapeDtypeStruct
    pad = pltpu.VMEM((length + 16, LANES), f32)
    sizes = dict(length=length, chunk=chunk, tiles=width // LANES)
    params = pltpu.CompilerParams(dimension_semantics=("arbitrary",))
    back = pl.pallas_call(
        functools.partial(conv_back_kernel, **sizes), grid=(inner // width,),
        in_specs=[tok, tok, tok, masks, taps, bias], out_specs=[tok, taps, bias],
        out_shape=[sds((length, inner), bf16), sds((2, KCONV, inner), f32), sds((2, inner), f32)],
        scratch_shapes=[pad] * 3, compiler_params=params, name="conv_back")
    return back


EPS = 1e-06
AXES = ("dp", "fsdp")
BIG = 1e30
LOG2E = 1.4426950408889634


def mm(a, b, dims):
    return lax.dot_general(a, b, (dims, ((), ())), preferred_element_type=f32)


def to_all(v):
    owners = lax.axis_size(AXES)
    return lax.all_to_all(jnp.broadcast_to(v[None], (owners,) + v.shape), AXES, 0, 0, tiled=True)


def gather0(v):
    return lax.all_gather(v, AXES, axis=0, tiled=True)


def tied(v, *after):
    return lax.optimization_barrier((v,) + after)[0]


def item_masks(ids):
    length = ids.shape[0]
    pad = jnp.full((KCONV - 1,), -1, ids.dtype)
    long = jnp.concatenate([pad, ids, pad])
    shifts = [-lag for lag in range(1, KCONV)] + list(range(1, KCONV))
    rows = [(long[KCONV - 1 + s:KCONV - 1 + s + length] == ids).astype(f32) for s in shifts]
    return jnp.broadcast_to(jnp.stack(rows)[:, :, None], (len(rows), length, LANES))


def body(tokens_in, condition, item_flags, grad_out, in_weight, out_weight, x_projection,
         dt_projection, conv_weight, conv_bias, dt_bias, decay_log, skip_gain, mod_weight, mod_bias):
    length, model = tokens_in.shape[1:]
    owners = lax.axis_size(AXES)
    me = lax.axis_index(AXES)
    inner = in_weight.shape[1] // 2
    own_model = in_weight.shape[0]
    rank = dt_projection.shape[1]

    own_inner = out_weight.shape[0]
    side = jnp.pad(jnp.swapaxes(dt_projection, 1, 2), ((0, 0), (0, 0), (0, LANES - rank)))
    pair = jnp.stack([x_projection, side])
    first = gather0(jnp.concatenate([in_weight[:, :inner], pair.reshape(-1, inner)], axis=0))

    cond = condition[0].astype(f32)
    act = jax.nn.silu(cond).astype(bf16)
    smalls = (act, conv_weight, conv_bias, dt_bias, decay_log, skip_gain, mod_bias)
    flat = jnp.concatenate([v.reshape(-1) for v in smalls])
    flat = jnp.pad(flat, (0, -flat.shape[0] % (8 * LANES)))
    everyone = to_all(flat.reshape(-1, LANES)).reshape(owners, -1)
    parts, at = [], 0
    for v in smalls:
        parts.append(everyone[:, at:at + v.size].reshape((owners,) + v.shape))
        at += v.size
    act_all = parts[0].reshape(owners * 2, model)
    join = lambda v, dim: jnp.moveaxis(v, 0, dim).reshape(
        v.shape[1:dim + 1] + (owners * v.shape[dim + 1],) + v.shape[dim + 2:]).astype(f32)
    conv_w, conv_b, dt_b = join(parts[1], 2), join(parts[2], 1), join(parts[3], 1)
    log_rate, skip = join(parts[4], 1), join(parts[5], 1)
    modb = parts[6].reshape(-1).astype(f32)

    act_own = lax.dynamic_slice(act_all, (0, me * own_model), (owners * 2, own_model))
    partial = mm(act_own, mod_weight, ((1,), (0,))).reshape(owners, 2, -1)
    mods = jnp.sum(lax.all_to_all(partial, AXES, 0, 0, tiled=True), axis=0) + modb
    flags = item_flags[0]
    ids = jnp.cumsum(flags, dtype=jnp.int32) - 1
    second = (ids == 1)[:, None]
    pick = lambda v: jnp.where(second, v[1], v[0])
    shift, scale, gate = (mods[:, i * model:(i + 1) * model] for i in range(3))
    masks = item_masks(ids)

    x = tokens_in[0].astype(f32)
    mean = jnp.mean(x, axis=1, keepdims=True)
    centered = x - mean
    inv = lax.rsqrt(jnp.mean(centered * centered, axis=1, keepdims=True) + EPS)
    normed = centered * inv
    hidden = (normed * (1.0 + pick(scale)) + pick(shift)).astype(bf16)
    first, hidden, masks = lax.optimization_barrier((first, hidden, masks))
    w_z = gather0(tied(in_weight[:, inner:], first))
    w_o = gather0(tied(out_weight, first))
    first = first.reshape(owners, -1, inner)
    w_x = first if own_model % 16 == 0 else first[:, :own_model].reshape(1, -1, inner)
    pair = jnp.moveaxis(first[:, own_model:].reshape(owners, 2, 2, own_inner, LANES), 0, 2)
    w_xp, w_dt = pair.reshape(2, 2, inner, LANES)
    g = grad_out[0].astype(f32)
    d_branch = (g * pick(gate)).astype(bf16)

    starts = flags.astype(f32)
    starts_b = jnp.concatenate([starts[1:], jnp.ones((1,), f32)])
    calls = [scan_calls(1, length, inner, bool(d)) for d in range(2)]
    project_conv, back_project = projection_calls(length, model, inner, 1 if w_x.shape[0] == 1 else owners)
    wide = lambda v: jnp.broadcast_to(v[None, :, :, None], (1, length, NST, LANES))
    tile = lambda v: jnp.tile(v, (1, SUB))[None]
    xs, *us = project_conv(hidden, w_x, masks, conv_w, conv_b)
    kept = []
    for d in range(2):
        u = us[d]
        proj = mm(u, w_xp[d], ((1,), (0,)))
        dt_low = proj.astype(bf16)
        b_m, c_m = proj[:, rank:rank + NST], proj[:, rank + NST:]
        delta = jax.nn.softplus(mm(dt_low, w_dt[d], ((1,), (1,))) + dt_b[d])
        rate = -jnp.exp(log_rate[d]).T
        rate2 = rate * LOG2E
        sb = jnp.broadcast_to((BIG * (starts_b if d else starts))[None, :, None], (1, length, LANES))
        b_wide = wide(b_m)
        y, ck = calls[d][0](delta[None], u[None], sb, b_wide, tile(c_m), rate2, skip[d][None])
        kept.append((u, dt_low, b_m, c_m, delta, rate, rate2, sb, b_wide, y[0], ck))
    gate_ahead, gate_back = gate_calls(length, model, inner)
    gated, silu_z, slope = gate_ahead(hidden, w_z, kept[0][9], kept[1][9])
    grad_out_w = mm(gated, d_branch, ((0,), (0,))).astype(bf16)
    d_branch, grad_out_w = lax.optimization_barrier((d_branch, grad_out_w))
    d_scan, d_z = gate_back(d_branch, w_o, silu_z, slope)
    grad_in_z = mm(hidden, d_z, ((0,), (0,))).astype(bf16)
    d_scan, grad_out_w, grad_in_z = lax.optimization_barrier((d_scan, grad_out_w, grad_in_z))
    over_dp = lambda v: lax.psum_scatter(v, "dp", scatter_dimension=0, tiled=True)
    over_fsdp = lambda v: lax.psum_scatter(v.reshape(-1, model), "fsdp", scatter_dimension=0, tiled=True)
    ranks = lax.axis_size("fsdp")
    halves = lambda v: [h.reshape(ranks, -1, model) for h in jnp.split(v, inner // model, axis=1)]
    joined = lambda v: jnp.concatenate(jnp.split(v, inner // model, axis=0), axis=1)
    grad_out_w = lax.psum_scatter(grad_out_w, AXES, scatter_dimension=0, tiled=True)
    grad_in_z = over_dp(grad_in_z)
    branch = mm(gated, w_o, ((1,), (0,)))
    block_out = (x + pick(gate) * branch).astype(bf16)
    d_gate = g * branch
    lane = lax.broadcasted_iota(jnp.int32, (1, LANES), 1)
    def by_owner(v, dim):
        shape = v.shape[:dim] + (owners, v.shape[dim] // owners) + v.shape[dim + 1:]
        return jnp.moveaxis(v.reshape(shape), dim, 0).astype(bf16)

    def send(values, dims):
        pieces = [by_owner(v, dim) for v, dim in zip(values, dims)]
        flat = jnp.concatenate([p.reshape(owners, -1) for p in pieces], axis=1)
        flat = jnp.pad(flat, ((0, 0), (0, -flat.shape[1] % (8 * LANES)))).reshape(owners, -1, LANES)
        return flat, [p.shape[1:] for p in pieces]

    def exchange(flat):
        return jnp.sum(lax.all_to_all(flat, AXES, 0, 0, tiled=True).astype(f32), axis=0).reshape(-1)

    def receive(own, shapes):
        out, at = [], 0
        for shape in shapes:
            count = 1
            for n in shape:
                count *= n
            out.append(own[at:at + count].reshape(shape))
            at += count
        return out

    d_us, sent = [], []
    carried = d_scan
    for d in range(2):
        u, dt_low, b_m, c_m, delta, rate, rate2, sb, b_wide, _, ck = kept[d]
        du, dr, db, dc, ga, gs, gb = calls[d][1](
            delta[None], u[None], sb, b_wide, wide(c_m), tile(b_m), carried[None], ck, rate, rate2,
            skip[d][None])
        dr = dr[0]
        if d == 1:
            dr, grad_in_z = lax.optimization_barrier((dr, grad_in_z))
        d_low = mm(dr, w_dt[d], ((1,), (0,)))
        d_proj = jnp.where(lane < rank, d_low, jnp.where(lane < rank + NST, db[0], dc[0])).astype(bf16)
        g_dt = mm(dr, dt_low, ((0,), (0,)))
        g_xp = mm(u, d_proj, ((0,), (0,)))
        flat, shapes = send((g_xp, g_dt, jnp.sum(gb, axis=0), ga.T, jnp.sum(gs, axis=0)), (0,) * 5)
        d_us.append(du[0] + mm(d_proj, w_xp[d], ((1,), (1,))))
        if d == 0:
            carried, flat = lax.optimization_barrier((carried, flat))
        else:
            d_us[1], flat = lax.optimization_barrier((d_us[1], flat))
        sent.append((flat, shapes))
    packed = jnp.concatenate([s[0].reshape(owners, -1) for s in sent], axis=1)
    span = sent[0][0].size // owners
    packed = jnp.pad(packed, ((0, 0), (0, -packed.shape[1] % (8 * model)))).reshape(-1, model)
    d_us[0], d_us[1], grad_out_w, packed = lax.optimization_barrier((d_us[0], d_us[1], grad_out_w, packed))
    packed = over_dp(packed)
    d_xs, g_cw, g_cb = conv_back_call(length, inner)(xs, d_us[0], d_us[1], masks, conv_w, conv_b)
    grad_in_x = mm(hidden, d_xs, ((0,), (0,))).astype(bf16)

    grad_in_x = over_dp(tied(grad_in_x, packed))
    flat, shapes = send((g_cw, g_cb), (2, 1))
    g_cw, g_cb = receive(exchange(flat), shapes)

    d_hidden = back_project(d_xs, d_z, w_x, w_z)
    scale_tok = 1.0 + pick(scale)
    d_n = d_hidden * scale_tok
    m1 = jnp.mean(d_n, axis=1, keepdims=True)
    m2 = jnp.mean(d_n * normed, axis=1, keepdims=True)
    grad_tokens = g + (d_n - m1 - normed * m2) * inv
    by_item = lambda v: jnp.stack([jnp.sum(jnp.where(second, 0.0, v), axis=0),
                                   jnp.sum(jnp.where(second, v, 0.0), axis=0)])
    d_mods = jnp.concatenate([by_item(d_hidden), by_item(d_hidden * normed), by_item(d_gate)], axis=1)
    d_mods_all = to_all(d_mods.astype(bf16)).reshape(owners * 2, -1)
    grad_mod_w = mm(act_own, d_mods_all, ((0,), (0,)))
    own_b = mod_bias.shape[0]
    grad_mod_b = jnp.sum(
        lax.dynamic_slice(d_mods_all, (0, me * own_b), (owners * 2, own_b)).astype(f32), axis=0)
    d_act = mm(d_mods_all, mod_weight, ((1,), (1,))).reshape(owners, 2, own_model)
    d_act = lax.all_to_all(d_act, AXES, 0, 0, tiled=True)
    grad_in_x, d_act, g_cw = lax.optimization_barrier((grad_in_x, d_act, g_cw))
    late = halves(grad_in_x) + halves(grad_in_z) + [packed.reshape(ranks, -1, model)]
    late = over_fsdp(jnp.concatenate(late, axis=1))
    count = own_model * (inner // model)
    grad_in = jnp.concatenate([joined(late[:count]), joined(late[count:2 * count])], axis=1).astype(f32)
    packed = late[2 * count:].reshape(-1)[:2 * span].astype(f32).reshape(2, -1)
    g_xp, g_dt, g_db, g_al, g_sk = [
        jnp.stack(v) for v in zip(*(receive(packed[d], sent[d][1]) for d in range(2)))]
    g_dt = jnp.swapaxes(g_dt[..., :rank], 1, 2)
    d_act = jnp.moveaxis(d_act, 0, 1).reshape(2, model)
    sc = jax.nn.sigmoid(cond)
    grad_cond = d_act * sc * (1.0 + cond * (1.0 - sc))
    return (block_out[None], grad_tokens[None], grad_cond[None], grad_in, grad_out_w.astype(f32), g_xp,
            g_dt, g_cw, g_cb, g_db, g_al, g_sk, grad_mod_w, grad_mod_b)


def solution(mesh):
    row3, row2, row1 = P(AXES, None, None), P(AXES, None), P(AXES)
    mid3, mid2, last3 = P(None, AXES, None), P(None, AXES), P(None, None, AXES)
    weights = (row2, row2, mid3, last3, last3, mid2, mid2, mid3, mid2, row2, row1)
    return jax.shard_map(
        body, mesh=mesh, in_specs=(row3, row3, row2, row3) + weights,
        out_specs=(row3, row3, row3) + weights, check_vma=False)
```

```python
import functools

import jax
import jax.numpy as jnp
from jax import lax
from jax.experimental import pallas as pl
from jax.experimental.pallas import tpu as pltpu
from jax.sharding import PartitionSpec as P

NST = 16
SUB = 16
KCONV = 4
LANES = 128
bf16 = jnp.bfloat16
f32 = jnp.float32


def split_hi_lo(v):
    hi = v.astype(bf16)
    lo = (v - hi.astype(f32)).astype(bf16)
    return jnp.concatenate([hi, lo], axis=0)


def block_diag(tiled):
    rows = lax.broadcasted_iota(jnp.int32, tiled.shape, 0) % SUB
    cols = lax.broadcasted_iota(jnp.int32, tiled.shape, 1) // NST
    return jnp.where(rows == cols, tiled, 0.0)


PAIR = 256


def fold(v):
    v = block_diag(v)
    v = v[:, :LANES] + v[:, LANES:]
    for by in (64, 32, 16):
        v = v + pltpu.roll(v, by, 1)
    return v


def same_state():
    rows = lax.broadcasted_iota(jnp.int32, (NST, SUB * NST), 0)
    cols = lax.broadcasted_iota(jnp.int32, (NST, SUB * NST), 1) % NST
    return jnp.where(rows == cols, 1.0, 0.0).astype(bf16)


def fwd_kernel(delta_ref, u_ref, sb_ref, bx_ref, ct_ref, a2_ref, skip_ref, y_ref, ck_ref,
               h_scr, dx_scr, du_scr, *, backwards, subs, width):
    lane0 = pl.multiple_of(pl.program_id(2) * width, width)

    @pl.when(pl.program_id(1) == 0)
    def _():
        h_scr[:, pl.ds(lane0, width)] = jnp.zeros((NST, width), f32)

    order = range(SUB - 1, -1, -1) if backwards else range(SUB)

    def sub_step(step, carry):
        sub = subs - 1 - step if backwards else step
        row0 = pl.multiple_of(sub * SUB, SUB)
        rows = pl.ds(row0, SUB)
        sb = sb_ref[rows, :]
        sb = jnp.concatenate([sb] * (PAIR // LANES), axis=1)
        c2 = split_hi_lo(block_diag(ct_ref[rows, :]))
        for p in range(width // PAIR):
            lanes = pl.ds(p * PAIR, PAIR)
            glob = pl.ds(lane0 + p * PAIR, PAIR)
            delta = delta_ref[rows, lanes]
            u = u_ref[rows, lanes].astype(f32)
            du_scr[:, lanes] = delta * u
            dx_scr[:, lanes] = delta + sb
            h = h_scr[:, glob]
            a2 = a2_ref[:, glob]
            ck_ref[sub, :, lanes] = h
            states = [None] * SUB
            for t in order:
                b = bx_ref[row0 + t]
                b = jnp.concatenate([b] * (PAIR // LANES), axis=1)
                h = jnp.exp2(dx_scr[pl.ds(t, 1), lanes] * a2) * h + du_scr[pl.ds(t, 1), lanes] * b
                states[t] = h.astype(bf16)
            h_scr[:, glob] = h
            y2 = jnp.dot(c2, jnp.concatenate(states, axis=0), preferred_element_type=f32)
            y_ref[rows, lanes] = y2[:SUB] + y2[SUB:] + skip_ref[:, glob] * u
        return carry

    lax.fori_loop(0, subs, sub_step, 0)


def bwd_kernel(delta_ref, u_ref, sb_ref, bx_ref, cx_ref, bt_ref, ds_ref, ck_ref, a_ref, a2_ref,
               skip_ref, du_out, dr_out, db_out, dc_out, ga_out, gs_out, gb_out,
               g_scr, dx_scr, du_scr, db_scr, dc_scr, *, backwards, subs, width):
    first = pl.program_id(1) == 0
    start = jnp.logical_and(first, pl.program_id(0) == 0)
    eg = pl.program_id(2)
    lane0 = pl.multiple_of(eg * width, width)
    wide = pl.ds(lane0, width)

    @pl.when(first)
    def _():
        g_scr[:, wide] = jnp.zeros((NST, width), f32)

    @pl.when(start)
    def _():
        ga_out[:, wide] = jnp.zeros((NST, width), f32)
        gs_out[:, wide] = jnp.zeros((SUB, width), f32)
        gb_out[:, wide] = jnp.zeros((SUB, width), f32)

    @pl.when(eg == 0)
    def _():
        db_scr[...] = jnp.zeros_like(db_scr)
        dc_scr[...] = jnp.zeros_like(dc_scr)

    order = list(range(SUB - 1, -1, -1) if backwards else range(SUB))
    nt = (((1,), (1,)), ((), ()))
    twice = lambda v: jnp.concatenate([v] * (PAIR // LANES), axis=1)

    def sub_step(step, carry):
        sub = step if backwards else subs - 1 - step
        row0 = pl.multiple_of(sub * SUB, SUB)
        rows = pl.ds(row0, SUB)
        sb = twice(sb_ref[rows, :])
        b2 = split_hi_lo(block_diag(bt_ref[rows, :]))
        ones = block_diag(jnp.ones((SUB, SUB * NST), f32)).astype(bf16)
        pick = same_state()
        db, dc = jnp.zeros((SUB, SUB * NST), f32), jnp.zeros((SUB, SUB * NST), f32)
        for p in range(width // PAIR):
            lanes = pl.ds(p * PAIR, PAIR)
            glob = pl.ds(lane0 + p * PAIR, PAIR)
            delta = delta_ref[rows, lanes]
            u = u_ref[rows, lanes].astype(f32)
            ds = ds_ref[rows, lanes]
            d_in = delta * u
            du_scr[:, lanes] = d_in
            dx_scr[:, lanes] = delta + sb
            a2 = a2_ref[:, glob]
            h = ck_ref[sub, :, lanes]
            decay, states, before = [None] * SUB, [None] * SUB, h.astype(bf16)
            prev = [None] * SUB
            for t in order:
                prev[t] = before
                decay[t] = jnp.exp2(dx_scr[pl.ds(t, 1), lanes] * a2)
                h = decay[t] * h + du_scr[pl.ds(t, 1), lanes] * twice(bx_ref[row0 + t])
                states[t] = before = h.astype(bf16)
            e2 = lax.dot_general(split_hi_lo(ds), jnp.concatenate(states, axis=0), nt,
                                 preferred_element_type=f32)
            dc = dc + (e2[:SUB] + e2[SUB:])
            a = a_ref[:, glob].astype(bf16)
            g = g_scr[:, glob]
            lams, rs, gas = [None] * SUB, [None] * SUB, [None] * SUB
            for t in reversed(order):
                lam = twice(cx_ref[row0 + t]) * ds_ref[pl.ds(row0 + t, 1), lanes] + g
                lams[t] = lam.astype(bf16)
                g = decay[t] * lam
                rs[t] = g.astype(bf16) * prev[t] * a
                gas[t] = rs[t] * jnp.broadcast_to(dx_scr[pl.ds(t, 1), lanes], (NST, PAIR)).astype(bf16)
            g_scr[:, glob] = g
            ga_out[:, glob] += jnp.dot(pick, jnp.concatenate(gas, axis=0), preferred_element_type=f32)
            lams = jnp.concatenate(lams, axis=0)
            s2 = jnp.dot(b2, lams, preferred_element_type=f32)
            s1 = s2[:SUB] + s2[SUB:]
            dd = jnp.dot(ones, jnp.concatenate(rs, axis=0), preferred_element_type=f32) + u * s1
            du_out[rows, lanes] = skip_ref[:, glob] * ds + delta * s1
            small = delta * (1.0 - delta * (0.5 - delta * (1.0 / 6.0)))
            sig = jnp.where(delta < 0.03, small, 1.0 - jnp.exp(-delta))
            dr = dd * sig
            dr_out[rows, lanes] = dr.astype(bf16)
            gb_out[:, glob] += dr
            gs_out[:, glob] += ds * u
            d2 = lax.dot_general(split_hi_lo(d_in), lams, nt, preferred_element_type=f32)
            db = db + (d2[:SUB] + d2[SUB:])
        db_scr[rows, :] += db
        dc_scr[rows, :] += dc
        return carry

    lax.fori_loop(0, subs, sub_step, 0)

    @pl.when(eg == pl.num_programs(2) - 1)
    def _():
        db_out[...] = fold(db_scr[...])
        dc_out[...] = fold(dc_scr[...])


def lane_groups(width_all, widths):
    for width in widths:
        if width_all % width == 0:
            return width
    return width_all


def scan_calls(rows, length, inner, backwards, tblock=128, width=None):
    width = width or lane_groups(inner, (3072, 1536, 1024, 512, 256))
    n_t, n_e, subs = length // tblock, inner // width, tblock // SUB
    params = pltpu.CompilerParams(dimension_semantics=("arbitrary",) * 3)

    def specs(flip):
        tb = (lambda i: n_t - 1 - i) if flip else (lambda i: i)
        tok = pl.BlockSpec((None, tblock, width), lambda r, i, e: (r, tb(i), e))
        lane = pl.BlockSpec((None, tblock, LANES), lambda r, i, e: (r, tb(i), 0))
        exp = pl.BlockSpec((None, tblock, NST, LANES), lambda r, i, e: (r, tb(i), 0, 0))
        til = pl.BlockSpec((None, tblock, SUB * NST), lambda r, i, e: (r, tb(i), 0))
        ck = pl.BlockSpec((None, subs, NST, width), lambda r, i, e: (r, tb(i), 0, e))
        full = pl.BlockSpec((NST, inner), lambda r, i, e: (0, 0))
        one = pl.BlockSpec((1, inner), lambda r, i, e: (0, 0))
        return tok, lane, exp, til, ck, full, one

    sds = jax.ShapeDtypeStruct
    tok, lane, exp, til, ck, full, one = specs(backwards)
    fwd = pl.pallas_call(
        functools.partial(fwd_kernel, backwards=backwards, subs=subs, width=width),
        grid=(rows, n_t, n_e),
        in_specs=[tok, tok, lane, exp, til, full, one],
        out_specs=[tok, ck],
        out_shape=[sds((rows, length, inner), f32), sds((rows, length // SUB, NST, inner), f32)],
        scratch_shapes=[pltpu.VMEM((NST, inner), f32)] + [pltpu.VMEM((SUB, width), f32)] * 2,
        compiler_params=params,
        name="scan_ahead_" + ("b" if backwards else "f"),
    )
    tok, lane, exp, til, ck, full, one = specs(not backwards)
    bwd = pl.pallas_call(
        functools.partial(bwd_kernel, backwards=backwards, subs=subs, width=width),
        grid=(rows, n_t, n_e),
        in_specs=[tok, tok, lane, exp, exp, til, tok, ck, full, full, one],
        out_specs=[tok, tok, lane, lane, full, full, full],
        out_shape=[sds((rows, length, inner), f32), sds((rows, length, inner), bf16),
                   sds((rows, length, LANES), f32), sds((rows, length, LANES), f32),
                   sds((NST, inner), f32), sds((SUB, inner), f32), sds((SUB, inner), f32)],
        scratch_shapes=[pltpu.VMEM((NST, inner), f32)] + [pltpu.VMEM((SUB, width), f32)] * 2
        + [pltpu.VMEM((tblock, SUB * NST), f32)] * 2,
        compiler_params=params,
        name="scan_back_" + ("b" if backwards else "f"),
    )
    return fwd, bwd


def conv_taps(pad_ref, row0, count, sign, masks_ref, lag):
    if lag == 0:
        return pad_ref[pl.ds(row0 + 8, count), :]
    side = 0 if sign > 0 else KCONV - 1
    return pad_ref[pl.ds(row0 + 8 - sign * lag, count), :] * masks_ref[side + lag - 1, pl.ds(row0, count), :]


def fill_padded(pad_ref, length):
    edge = jnp.zeros((8, LANES), f32)
    pad_ref[pl.ds(0, 8), :] = edge
    pad_ref[pl.ds(8 + length, 8), :] = edge


def project_conv_kernel(h_ref, wts_ref, masks_ref, w_ref, b_ref, x_ref, u0_ref, u1_ref, pad_scr,
                        *, length, chunk, width):
    for half in range(width // PAIR):
        cols = pl.ds(half * PAIR, PAIR)
        wts = wts_ref[:, :, cols].reshape(h_ref.shape[1], PAIR)
        x_ref[:, cols] = jnp.dot(h_ref[...], wts, preferred_element_type=f32)
    for tile in range(width // LANES):
        lanes = pl.ds(tile * LANES, LANES)
        pad = pad_scr.at[tile % 2]
        fill_padded(pad, length)
        pad[pl.ds(8, length), :] = x_ref[:, lanes]
        for row0 in range(0, length, chunk):
            for d, (sign, out) in enumerate(((1, u0_ref), (-1, u1_ref))):
                pre = b_ref[d:d + 1, lanes]
                for lag in range(KCONV):
                    tap = conv_taps(pad, row0, chunk, sign, masks_ref, lag)
                    pre = pre + w_ref[d, lag:lag + 1, lanes] * tap
                out[pl.ds(row0, chunk), lanes] = (pre * jax.nn.sigmoid(pre)).astype(bf16)


def back_project_kernel(dx_ref, dz_ref, wx_ref, wz_ref, out_ref, *, width):
    @pl.when(pl.program_id(0) == 0)
    def _():
        out_ref[...] = jnp.zeros_like(out_ref)

    nt = (((1,), (1,)), ((), ()))
    wx = wx_ref[...].reshape(out_ref.shape[1], width)
    out_ref[...] += (lax.dot_general(dx_ref[...], wx, nt, preferred_element_type=f32)
                     + lax.dot_general(dz_ref[...], wz_ref[...], nt, preferred_element_type=f32))


def conv_back_kernel(x_ref, du0_ref, du1_ref, masks_ref, w_ref, b_ref, dx_ref, gw_ref, gb_ref,
                     pad_scr, dp0_scr, dp1_scr, *, length, chunk, tiles):
    both = ((1, du0_ref, dp0_scr), (-1, du1_ref, dp1_scr))
    for tile in range(tiles):
        lanes = pl.ds(tile * LANES, LANES)
        for ref in (pad_scr, dp0_scr, dp1_scr):
            fill_padded(ref, length)
        pad_scr[pl.ds(8, length), :] = x_ref[:, lanes]
        for d, (sign, du_ref, dp_scr) in enumerate(both):
            sums = [jnp.zeros((8, LANES), f32) for _ in range(KCONV + 1)]
            for row0 in range(0, length, chunk):
                taps = [conv_taps(pad_scr, row0, chunk, sign, masks_ref, lag) for lag in range(KCONV)]
                pre = b_ref[d:d + 1, lanes]
                for lag in range(KCONV):
                    pre = pre + w_ref[d, lag:lag + 1, lanes] * taps[lag]
                sg = jax.nn.sigmoid(pre)
                d_pre = du_ref[pl.ds(row0, chunk), lanes] * (sg * (1.0 + pre * (1.0 - sg)))
                dp_scr[pl.ds(row0 + 8, chunk), :] = d_pre
                for lag in range(KCONV + 1):
                    term = d_pre * taps[lag] if lag < KCONV else d_pre
                    sums[lag] = sums[lag] + jnp.sum(term.reshape(chunk // 8, 8, LANES), axis=0)
            for lag in range(KCONV):
                gw_ref[d, lag:lag + 1, lanes] = jnp.sum(sums[lag], axis=0, keepdims=True)
            gb_ref[d:d + 1, lanes] = jnp.sum(sums[KCONV], axis=0, keepdims=True)
        for row0 in range(0, length, chunk):
            total = jnp.zeros((chunk, LANES), f32)
            for d, (sign, _, dp_scr) in enumerate(both):
                for lag in range(KCONV):
                    total = total + w_ref[d, lag:lag + 1, lanes] * conv_taps(
                        dp_scr, row0, chunk, -sign, masks_ref, lag)
            dx_ref[pl.ds(row0, chunk), lanes] = total.astype(bf16)


def gate_kernel(h_ref, wz_ref, y0_ref, y1_ref, gated_ref, silu_ref, slope_ref, *, length, chunk):
    silu_ref[...] = jnp.dot(h_ref[...], wz_ref[...], preferred_element_type=f32)
    for row0 in range(0, length, chunk):
        rows = pl.ds(row0, chunk)
        z = silu_ref[rows, :]
        both = y0_ref[rows, :] + y1_ref[rows, :]
        sig = jax.nn.sigmoid(z)
        silu = z * sig
        gated_ref[rows, :] = (both * silu).astype(bf16)
        silu_ref[rows, :] = silu
        slope_ref[rows, :] = both * sig * (1.0 + z * (1.0 - sig))


def gate_back_kernel(g_ref, wo_ref, silu_ref, slope_ref, ds_ref, dz_ref, *, length, chunk):
    ds_ref[...] = lax.dot_general(g_ref[...], wo_ref[...], (((1,), (1,)), ((), ())),
                                  preferred_element_type=f32)
    for row0 in range(0, length, chunk):
        rows = pl.ds(row0, chunk)
        d_gated = ds_ref[rows, :]
        ds_ref[rows, :] = d_gated * silu_ref[rows, :]
        dz_ref[rows, :] = (d_gated * slope_ref[rows, :]).astype(bf16)


def gate_calls(length, model, inner, width=384, chunk=32):
    if inner % width:
        width = PAIR
    tok = pl.BlockSpec((length, width), lambda e: (0, e))
    every = pl.BlockSpec((length, model), lambda e: (0, 0))
    low = jax.ShapeDtypeStruct((length, inner), bf16)
    high = jax.ShapeDtypeStruct((length, inner), f32)
    params = pltpu.CompilerParams(dimension_semantics=("arbitrary",))
    ahead = pl.pallas_call(
        functools.partial(gate_kernel, length=length, chunk=chunk), grid=(inner // width,),
        in_specs=[every, pl.BlockSpec((model, width), lambda e: (0, e)), tok, tok],
        out_specs=[tok, tok, tok], out_shape=[low, high, high], compiler_params=params, name="gate")
    back = pl.pallas_call(
        functools.partial(gate_back_kernel, length=length, chunk=chunk), grid=(inner // width,),
        in_specs=[every, pl.BlockSpec((width, model), lambda e: (e, 0)), tok, tok],
        out_specs=[tok, tok], out_shape=[high, low], compiler_params=params, name="gate_back")
    return ahead, back


def projection_calls(length, model, inner, blocks, width=512, chunk=64):
    if inner % width:
        width = PAIR
    rows = model // blocks
    tok = pl.BlockSpec((length, width), lambda e: (0, e))
    every = pl.BlockSpec((length, model), lambda e: (0, 0))
    wts = pl.BlockSpec((blocks, rows, width), lambda e: (0, 0, e))
    flat = pl.BlockSpec((model, width), lambda e: (0, e))
    masks = pl.BlockSpec((2 * (KCONV - 1), length, LANES), lambda e: (0, 0, 0))
    taps = pl.BlockSpec((2, KCONV, width), lambda e: (0, 0, e))
    bias = pl.BlockSpec((2, width), lambda e: (0, e))
    sds = jax.ShapeDtypeStruct
    params = pltpu.CompilerParams(dimension_semantics=("arbitrary",))
    ahead = pl.pallas_call(
        functools.partial(project_conv_kernel, length=length, chunk=chunk, width=width),
        grid=(inner // width,), in_specs=[every, wts, masks, taps, bias], out_specs=[tok, tok, tok],
        out_shape=[sds((length, inner), f32)] + [sds((length, inner), bf16)] * 2,
        scratch_shapes=[pltpu.VMEM((2, length + 16, LANES), f32)], compiler_params=params,
        name="project_conv")
    back = pl.pallas_call(
        functools.partial(back_project_kernel, width=width), grid=(inner // width,),
        in_specs=[tok, tok, wts, flat], out_specs=every,
        out_shape=sds((length, model), f32), compiler_params=params, name="back_project")
    return ahead, back


def conv_back_call(length, inner, width=256, chunk=64):
    if inner % width:
        width = LANES
    tok = pl.BlockSpec((length, width), lambda e: (0, e))
    masks = pl.BlockSpec((2 * (KCONV - 1), length, LANES), lambda e: (0, 0, 0))
    taps = pl.BlockSpec((2, KCONV, width), lambda e: (0, 0, e))
    bias = pl.BlockSpec((2, width), lambda e: (0, e))
    sds = jax.ShapeDtypeStruct
    pad = pltpu.VMEM((length + 16, LANES), f32)
    sizes = dict(length=length, chunk=chunk, tiles=width // LANES)
    params = pltpu.CompilerParams(dimension_semantics=("arbitrary",))
    back = pl.pallas_call(
        functools.partial(conv_back_kernel, **sizes), grid=(inner // width,),
        in_specs=[tok, tok, tok, masks, taps, bias], out_specs=[tok, taps, bias],
        out_shape=[sds((length, inner), bf16), sds((2, KCONV, inner), f32), sds((2, inner), f32)],
        scratch_shapes=[pad] * 3, compiler_params=params, name="conv_back")
    return back


EPS = 1e-06
AXES = ("dp", "fsdp")
BIG = 1e30
LOG2E = 1.4426950408889634


def mm(a, b, dims):
    return lax.dot_general(a, b, (dims, ((), ())), preferred_element_type=f32)


def to_all(v):
    owners = lax.axis_size(AXES)
    return lax.all_to_all(jnp.broadcast_to(v[None], (owners,) + v.shape), AXES, 0, 0, tiled=True)


def gather0(v):
    return lax.all_gather(v, AXES, axis=0, tiled=True)


def tied(v, *after):
    return lax.optimization_barrier((v,) + after)[0]


def item_masks(ids):
    length = ids.shape[0]
    pad = jnp.full((KCONV - 1,), -1, ids.dtype)
    long = jnp.concatenate([pad, ids, pad])
    shifts = [-lag for lag in range(1, KCONV)] + list(range(1, KCONV))
    rows = [(long[KCONV - 1 + s:KCONV - 1 + s + length] == ids).astype(f32) for s in shifts]
    return jnp.broadcast_to(jnp.stack(rows)[:, :, None], (len(rows), length, LANES))


def body(tokens_in, condition, item_flags, grad_out, in_weight, out_weight, x_projection,
         dt_projection, conv_weight, conv_bias, dt_bias, decay_log, skip_gain, mod_weight, mod_bias):
    length, model = tokens_in.shape[1:]
    owners = lax.axis_size(AXES)
    me = lax.axis_index(AXES)
    inner = in_weight.shape[1] // 2
    own_model = in_weight.shape[0]
    rank = dt_projection.shape[1]

    own_inner = out_weight.shape[0]
    side = jnp.pad(jnp.swapaxes(dt_projection, 1, 2), ((0, 0), (0, 0), (0, LANES - rank)))
    pair = jnp.stack([x_projection, side])
    first = gather0(jnp.concatenate([in_weight[:, :inner], pair.reshape(-1, inner)], axis=0))

    cond = condition[0].astype(f32)
    act = jax.nn.silu(cond).astype(bf16)
    smalls = (act, conv_weight, conv_bias, dt_bias, decay_log, skip_gain, mod_bias)
    flat = jnp.concatenate([v.reshape(-1) for v in smalls])
    flat = jnp.pad(flat, (0, -flat.shape[0] % (8 * LANES)))
    everyone = to_all(flat.reshape(-1, LANES)).reshape(owners, -1)
    parts, at = [], 0
    for v in smalls:
        parts.append(everyone[:, at:at + v.size].reshape((owners,) + v.shape))
        at += v.size
    act_all = parts[0].reshape(owners * 2, model)
    join = lambda v, dim: jnp.moveaxis(v, 0, dim).reshape(
        v.shape[1:dim + 1] + (owners * v.shape[dim + 1],) + v.shape[dim + 2:]).astype(f32)
    conv_w, conv_b, dt_b = join(parts[1], 2), join(parts[2], 1), join(parts[3], 1)
    log_rate, skip = join(parts[4], 1), join(parts[5], 1)
    modb = parts[6].reshape(-1).astype(f32)

    act_own = lax.dynamic_slice(act_all, (0, me * own_model), (owners * 2, own_model))
    partial = mm(act_own, mod_weight, ((1,), (0,))).astype(bf16).reshape(owners, 2, -1)
    mods = jnp.sum(lax.all_to_all(partial, AXES, 0, 0, tiled=True).astype(f32), axis=0) + modb
    flags = item_flags[0]
    ids = jnp.cumsum(flags, dtype=jnp.int32) - 1
    second = (ids == 1)[:, None]
    pick = lambda v: jnp.where(second, v[1], v[0])
    shift, scale, gate = (mods[:, i * model:(i + 1) * model] for i in range(3))
    masks = item_masks(ids)

    x = tokens_in[0].astype(f32)
    mean = jnp.mean(x, axis=1, keepdims=True)
    centered = x - mean
    inv = lax.rsqrt(jnp.mean(centered * centered, axis=1, keepdims=True) + EPS)
    normed = centered * inv
    hidden = (normed * (1.0 + pick(scale)) + pick(shift)).astype(bf16)
    first, hidden, masks = lax.optimization_barrier((first, hidden, masks))
    w_z = gather0(tied(in_weight[:, inner:], first))
    w_o = gather0(tied(out_weight, first))
    first = first.reshape(owners, -1, inner)
    w_x = first if own_model % 16 == 0 else first[:, :own_model].reshape(1, -1, inner)
    pair = jnp.moveaxis(first[:, own_model:].reshape(owners, 2, 2, own_inner, LANES), 0, 2)
    w_xp, w_dt = pair.reshape(2, 2, inner, LANES)
    g = grad_out[0].astype(f32)
    d_branch = (g * pick(gate)).astype(bf16)

    starts = flags.astype(f32)
    starts_b = jnp.concatenate([starts[1:], jnp.ones((1,), f32)])
    calls = [scan_calls(1, length, inner, bool(d)) for d in range(2)]
    project_conv, back_project = projection_calls(length, model, inner, 1 if w_x.shape[0] == 1 else owners)
    wide = lambda v: jnp.broadcast_to(v[None, :, :, None], (1, length, NST, LANES))
    tile = lambda v: jnp.tile(v, (1, SUB))[None]
    xs, *us = project_conv(hidden, w_x, masks, conv_w, conv_b)
    kept = []
    for d in range(2):
        u = us[d]
        proj = mm(u, w_xp[d], ((1,), (0,)))
        dt_low = proj.astype(bf16)
        b_m, c_m = proj[:, rank:rank + NST], proj[:, rank + NST:]
        delta = jax.nn.softplus(mm(dt_low, w_dt[d], ((1,), (1,))) + dt_b[d])
        rate = -jnp.exp(log_rate[d]).T
        rate2 = rate * LOG2E
        sb = jnp.broadcast_to((BIG * (starts_b if d else starts))[None, :, None], (1, length, LANES))
        b_wide = wide(b_m)
        y, ck = calls[d][0](delta[None], u[None], sb, b_wide, tile(c_m), rate2, skip[d][None])
        kept.append((u, dt_low, b_m, c_m, delta, rate, rate2, sb, b_wide, y[0], ck))
    gate_ahead, gate_back = gate_calls(length, model, inner)
    gated, silu_z, slope = gate_ahead(hidden, w_z, kept[0][9], kept[1][9])
    grad_out_w = mm(gated, d_branch, ((0,), (0,))).astype(bf16)
    d_branch, grad_out_w = lax.optimization_barrier((d_branch, grad_out_w))
    d_scan, d_z = gate_back(d_branch, w_o, silu_z, slope)
    grad_in_z = mm(hidden, d_z, ((0,), (0,))).astype(bf16)
    d_scan, grad_out_w, grad_in_z = lax.optimization_barrier((d_scan, grad_out_w, grad_in_z))
    over_dp = lambda v: lax.psum_scatter(v, "dp", scatter_dimension=0, tiled=True)
    over_fsdp = lambda v: lax.psum_scatter(v.reshape(-1, model), "fsdp", scatter_dimension=0, tiled=True)
    ranks = lax.axis_size("fsdp")
    halves = lambda v: [h.reshape(ranks, -1, model) for h in jnp.split(v, inner // model, axis=1)]
    joined = lambda v: jnp.concatenate(jnp.split(v, inner // model, axis=0), axis=1)
    grad_out_w = lax.psum_scatter(grad_out_w, AXES, scatter_dimension=0, tiled=True)
    grad_in_z = over_dp(grad_in_z)
    branch = mm(gated, w_o, ((1,), (0,)))
    block_out = (x + pick(gate) * branch).astype(bf16)
    d_gate = g * branch
    lane = lax.broadcasted_iota(jnp.int32, (1, LANES), 1)
    def by_owner(v, dim):
        shape = v.shape[:dim] + (owners, v.shape[dim] // owners) + v.shape[dim + 1:]
        return jnp.moveaxis(v.reshape(shape), dim, 0).astype(bf16)

    def send(values, dims):
        pieces = [by_owner(v, dim) for v, dim in zip(values, dims)]
        flat = jnp.concatenate([p.reshape(owners, -1) for p in pieces], axis=1)
        flat = jnp.pad(flat, ((0, 0), (0, -flat.shape[1] % (8 * LANES)))).reshape(owners, -1, LANES)
        return flat, [p.shape[1:] for p in pieces]

    def exchange(flat):
        return jnp.sum(lax.all_to_all(flat, AXES, 0, 0, tiled=True).astype(f32), axis=0).reshape(-1)

    def receive(own, shapes):
        out, at = [], 0
        for shape in shapes:
            count = 1
            for n in shape:
                count *= n
            out.append(own[at:at + count].reshape(shape))
            at += count
        return out

    d_us, sent = [], []
    carried = d_scan
    for d in range(2):
        u, dt_low, b_m, c_m, delta, rate, rate2, sb, b_wide, _, ck = kept[d]
        du, dr, db, dc, ga, gs, gb = calls[d][1](
            delta[None], u[None], sb, b_wide, wide(c_m), tile(b_m), carried[None], ck, rate, rate2,
            skip[d][None])
        dr = dr[0]
        if d == 1:
            dr, grad_in_z = lax.optimization_barrier((dr, grad_in_z))
        d_low = mm(dr, w_dt[d], ((1,), (0,)))
        d_proj = jnp.where(lane < rank, d_low, jnp.where(lane < rank + NST, db[0], dc[0])).astype(bf16)
        g_dt = mm(dr, dt_low, ((0,), (0,)))
        g_xp = mm(u, d_proj, ((0,), (0,)))
        flat, shapes = send((g_xp, g_dt, jnp.sum(gb, axis=0), ga.T, jnp.sum(gs, axis=0)), (0,) * 5)
        d_us.append((du[0], d_proj))
        if d == 0:
            carried, flat = lax.optimization_barrier((carried, flat))
        sent.append((flat, shapes))
    packed = jnp.concatenate([s[0].reshape(owners, -1) for s in sent], axis=1)
    span = sent[0][0].size // owners
    packed = jnp.pad(packed, ((0, 0), (0, -packed.shape[1] % (8 * model)))).reshape(-1, model)
    d_us, grad_out_w, packed = lax.optimization_barrier((d_us, grad_out_w, packed))
    d_us = [du + mm(d_proj, w_xp[d], ((1,), (1,))) for d, (du, d_proj) in enumerate(d_us)]
    packed = over_dp(packed)
    d_xs, g_cw, g_cb = conv_back_call(length, inner)(xs, d_us[0], d_us[1], masks, conv_w, conv_b)
    grad_in_x = mm(hidden, d_xs, ((0,), (0,))).astype(bf16)

    grad_in_x = over_dp(tied(grad_in_x, packed))
    flat, shapes = send((g_cw, g_cb), (2, 1))
    g_cw, g_cb = receive(exchange(flat), shapes)

    d_hidden = back_project(d_xs, d_z, w_x, w_z)
    scale_tok = 1.0 + pick(scale)
    d_n = d_hidden * scale_tok
    m1 = jnp.mean(d_n, axis=1, keepdims=True)
    m2 = jnp.mean(d_n * normed, axis=1, keepdims=True)
    grad_tokens = g + (d_n - m1 - normed * m2) * inv
    by_item = lambda v: jnp.stack([jnp.sum(jnp.where(second, 0.0, v), axis=0),
                                   jnp.sum(jnp.where(second, v, 0.0), axis=0)])
    d_mods = jnp.concatenate([by_item(d_hidden), by_item(d_hidden * normed), by_item(d_gate)], axis=1)
    d_mods_all = to_all(d_mods.astype(bf16)).reshape(owners * 2, -1)
    grad_mod_w = mm(act_own, d_mods_all, ((0,), (0,)))
    own_b = mod_bias.shape[0]
    grad_mod_b = jnp.sum(
        lax.dynamic_slice(d_mods_all, (0, me * own_b), (owners * 2, own_b)).astype(f32), axis=0)
    d_act = mm(d_mods_all, mod_weight, ((1,), (1,))).reshape(owners, 2, own_model)
    d_act = lax.all_to_all(d_act, AXES, 0, 0, tiled=True)
    grad_in_x, d_act, g_cw = lax.optimization_barrier((grad_in_x, d_act, g_cw))
    late = halves(grad_in_x) + halves(grad_in_z) + [packed.reshape(ranks, -1, model)]
    late = over_fsdp(jnp.concatenate(late, axis=1))
    count = own_model * (inner // model)
    grad_in = jnp.concatenate([joined(late[:count]), joined(late[count:2 * count])], axis=1).astype(f32)
    packed = late[2 * count:].reshape(-1)[:2 * span].astype(f32).reshape(2, -1)
    g_xp, g_dt, g_db, g_al, g_sk = [
        jnp.stack(v) for v in zip(*(receive(packed[d], sent[d][1]) for d in range(2)))]
    g_dt = jnp.swapaxes(g_dt[..., :rank], 1, 2)
    d_act = jnp.moveaxis(d_act, 0, 1).reshape(2, model)
    sc = jax.nn.sigmoid(cond)
    grad_cond = d_act * sc * (1.0 + cond * (1.0 - sc))
    return (block_out[None], grad_tokens[None], grad_cond[None], grad_in, grad_out_w.astype(f32), g_xp,
            g_dt, g_cw, g_cb, g_db, g_al, g_sk, grad_mod_w, grad_mod_b)


def solution(mesh):
    row3, row2, row1 = P(AXES, None, None), P(AXES, None), P(AXES)
    mid3, mid2, last3 = P(None, AXES, None), P(None, AXES), P(None, None, AXES)
    weights = (row2, row2, mid3, last3, last3, mid2, mid2, mid3, mid2, row2, row1)
    return jax.shard_map(
        body, mesh=mesh, in_specs=(row3, row3, row2, row3) + weights,
        out_specs=(row3, row3, row3) + weights, check_vma=False)
```
